32 devices in a mesh: req: 8 (over y, x, core), kvh: 4 (over z).
Axes of the slice: x: 2, y: 2, z: 4, core: 2. Of those that a mesh axis runs over, the one named last changes fastest.
Arguments:
- queries: bfloat16 [128, 8192], P('req', 'kvh'), may hold values from -150 to 150
- corpus_keys: bfloat16 [32768, 1024], P('req', 'kvh'), may hold values from -6 to 6
- corpus_values: bfloat16 [32768, 1024], P('req', 'kvh'), may hold values from -6 to 6
- task_keys: bfloat16 [16384, 1024], P('req', 'kvh'), may hold values from -7 to 7
- task_values: bfloat16 [16384, 1024], P('req', 'kvh'), may hold values from -6 to 6
- history_keys: bfloat16 [65536, 1024], P('req', 'kvh'), may hold values from -8 to 8
- history_values: bfloat16 [65536, 1024], P('req', 'kvh'), may hold values from -6 to 6
- history_lengths: int32 [128], P('req'), may hold values from 1 to 512, as said below
- task_of: int32 [128], replicated, may hold values from 0 to 3
- out_weight: bfloat16 [8192, 8192], P('kvh'), may hold values from -0.0625 to 0.0625
Outputs:
- mixed: bfloat16 [128, 8192], P('req', 'kvh')
The draws below stay inside these ranges and needn't reach their ends.
Inputs may be any that keep to these rules, and one draw needn't show every extreme that they name: `history_lengths`: each request's live history rows are its first rows; some request has 512 of them in every draw.
All inputs are finite; a program needn't handle non-finite values.
Results may differ from the reference program's by a relative error of at most 0.014.
Values may be sent and summed in bfloat16 or wider, within the bound.
No kernel may reach another device: no remote copies, remote signals or barrier semaphores. Data moves between devices by JAX's collectives and lax.ppermute only.
A program may use at most 128 MiB of HBM per device.

```python
import math
import jax
import jax.numpy as jnp
import numpy as np
from jax import lax

D = 8192
HQ = 64
KVH = 8
HD = 128
TASK_DEV = 2048
HIST = 512
HOLDERS = 2
REQUESTS = 128
CORPUS = 32768
TASKS = 4
TASK_TOKENS = 16384


def draw_queries(key, part):
    values = jnp.clip(jax.random.normal(key, (REQUESTS, HQ * HD), jnp.float32), -6.0, 6.0) * 3.0
    return values.astype(jnp.bfloat16)


def draw_history_lengths(key, part):
    lengths = jax.random.randint(key, (REQUESTS,), 1, HIST + 1, jnp.int32)
    chosen = jax.random.randint(jax.random.fold_in(key, 7), (), 0, REQUESTS, jnp.int32)
    return lengths.at[chosen].set(HIST)


def place_ends(result, stream_key, low, top_value):
    shape = result.shape
    place = [jax.random.randint(jax.random.fold_in(stream_key, axis), (), 0, shape[axis]) for axis in range(len(shape))]
    result = result.at[tuple(place)].set(low)
    longest = shape.index(max(shape))
    place[longest] = (place[longest] + 1) % shape[longest]
    return result.at[tuple(place)].set(top_value)


def level_of(key, extent, pieces, smallest, largest):
    level = 1.0
    for dim, blocks in pieces:
        steps = jax.random.uniform(jax.random.fold_in(jax.random.fold_in(key, 6), dim), (blocks,), jnp.float32, smallest / len(pieces), largest / len(pieces))
        level = level * jnp.repeat(jnp.exp(steps), extent[dim] // blocks).reshape((-1,) + (1,) * (len(extent) - 1 - dim))
    return level


def rank_table(number_of, skew):
    loads = [(1 << 20) // math.isqrt(rank ** skew) + 1 for rank in range(1, number_of + 1)]
    width = 1 + sum(loads) // (1 << 30)
    return np.cumsum(np.array([max(1, weight // width) for weight in loads]))


def ranked(own_key, dims, amount, skew):
    listing = rank_table(amount, skew)
    pick = jax.random.randint(jax.random.fold_in(own_key, 1), dims, 0, int(listing[amount - 1]))
    grade = jnp.searchsorted(jnp.asarray(listing, jnp.int32), pick, side="right")
    return jax.random.permutation(jax.random.fold_in(own_key, 2), amount)[grade].astype(jnp.int32)


def scatter_about(stream_key, shape, width, limit, cuts=(), kind=jnp.bfloat16):
    values = jax.random.normal(stream_key, shape, jnp.float32) * width
    if len(cuts) > 0:
        values = level_of(stream_key, shape, cuts, -0.22, 0.18) * values
    return jnp.clip(values, min=-limit, max=limit).astype(kind)


def setup_inputs(seed: int = 0) -> dict:
    key_of = jax.random.split(jax.random.key(seed), 11)
    queries = draw_queries(jax.random.fold_in(key_of[10], 71), 0)
    corpus_keys = scatter_about(key_of[1], (CORPUS, KVH * HD), 1.0, 6.0, ((0, 8), (1, 4)))
    corpus_values = scatter_about(key_of[2], (CORPUS, KVH * HD), 1.0, 6.0, ((0, 8), (1, 4)))
    task_keys = scatter_about(key_of[3], (TASK_TOKENS, KVH * HD), 1.15, 7.0, ((0, 8), (1, 4)))
    task_values = scatter_about(key_of[4], (TASK_TOKENS, KVH * HD), 1.0, 6.0, ((0, 8), (1, 4)))
    history_keys = scatter_about(key_of[5], (REQUESTS * HIST, KVH * HD), 1.35, 8.0, ((0, 8), (1, 4)))
    history_values = scatter_about(key_of[6], (REQUESTS * HIST, KVH * HD), 1.0, 6.0, ((0, 8), (1, 4)))
    history_lengths = draw_history_lengths(jax.random.fold_in(key_of[10], 71), 0)
    task_of = place_ends(ranked(key_of[8], (REQUESTS,), TASKS, 2), jax.random.fold_in(key_of[8], 3), 0, TASKS - 1).astype(jnp.int32)
    out_weight = scatter_about(key_of[9], (HQ * HD, D), (HQ * HD) ** -0.5, 0.0625, ((0, 4),))
    return {"queries": queries, "corpus_keys": corpus_keys, "corpus_values": corpus_values, "task_keys": task_keys, "task_values": task_values, "history_keys": history_keys, "history_values": history_values, "history_lengths": history_lengths, "task_of": task_of, "out_weight": out_weight}


def reference(queries, corpus_keys, corpus_values, task_keys, task_values, history_keys, history_values, history_lengths, task_of, out_weight):
    group = HQ // KVH
    scale = 1.0 / math.sqrt(HD)
    span = HOLDERS * TASK_DEV
    corpus_kf = corpus_keys.astype(jnp.float32).reshape(CORPUS, KVH, HD)
    corpus_vf = corpus_values.astype(jnp.float32).reshape(CORPUS, KVH, HD)
    task_kf = task_keys.astype(jnp.float32).reshape(TASK_TOKENS, KVH, HD)
    task_vf = task_values.astype(jnp.float32).reshape(TASK_TOKENS, KVH, HD)

    def rounded(weights):
        narrow = lax.optimization_barrier(weights.astype(jnp.bfloat16))
        return narrow.astype(jnp.float32)

    def single(index):
        query = lax.dynamic_slice_in_dim(queries, index, 1, 0).astype(jnp.float32).reshape(KVH, group, HD)
        start = (task_of[index] * span).astype(jnp.int32)
        tkeys = lax.dynamic_slice_in_dim(task_kf, start, span, 0)
        tvals = lax.dynamic_slice_in_dim(task_vf, start, span, 0)
        hstart = (index * HIST).astype(jnp.int32)
        hkeys = lax.dynamic_slice_in_dim(history_keys, hstart, HIST, 0).astype(jnp.float32).reshape(HIST, KVH, HD)
        hvals = lax.dynamic_slice_in_dim(history_values, hstart, HIST, 0).astype(jnp.float32).reshape(HIST, KVH, HD)
        first = jnp.einsum('kgd,skd->kgs', query, corpus_kf) * scale
        second = jnp.einsum('kgd,skd->kgs', query, tkeys) * scale
        third = jnp.einsum('kgd,skd->kgs', query, hkeys) * scale
        valid = jnp.arange(HIST, dtype=jnp.int32) < history_lengths[index]
        third = jnp.where(valid, third, -jnp.inf)
        top = jnp.maximum(jnp.maximum(lax.optimization_barrier(jnp.max(first, -1)), lax.optimization_barrier(jnp.max(second, -1))), lax.optimization_barrier(jnp.max(third, -1)))
        pone = jnp.exp(first - top[..., None])
        ptwo = jnp.exp(second - top[..., None])
        pthree = jnp.where(valid, jnp.exp(third - top[..., None]), 0.0)
        total = lax.optimization_barrier(jnp.sum(pone, -1)) + lax.optimization_barrier(jnp.sum(ptwo, -1)) + lax.optimization_barrier(jnp.sum(pthree, -1))
        summed = jnp.einsum('kgs,skd->kgd', rounded(pone), corpus_vf)
        summed = summed + jnp.einsum('kgs,skd->kgd', rounded(ptwo), tvals)
        summed = summed + jnp.einsum('kgs,skd->kgd', rounded(pthree), hvals)
        return (summed / total[..., None]).reshape(HQ * HD).astype(jnp.bfloat16)
    attended = lax.map(single, jnp.arange(REQUESTS, dtype=jnp.int32))
    return jnp.dot(attended, out_weight, preferred_element_type=jnp.float32).astype(jnp.bfloat16)
```

```python
import functools
import math

import jax
import jax.numpy as jnp
from jax import lax
from jax.experimental import pallas as pl
from jax.experimental.pallas import tpu as pltpu
from jax.sharding import PartitionSpec as P

HD = 128
HOLDERS = 2
LOG2 = math.log2(math.e) / math.sqrt(HD)
BIG = 1e30
COLS = 256
STEP = 1024
SUB = 512
AUG = 144
BF = jnp.bfloat16
F32 = jnp.float32


def dot_nt(a, b):
    return lax.dot_general(a, b, (((1,), (1,)), ((), ())), preferred_element_type=F32)


def dot_nn(a, b):
    return lax.dot_general(a, b, (((1,), (0,)), ((), ())), preferred_element_type=F32)


def split3(x):
    first = x.astype(BF)
    rest = x - first.astype(F32)
    second = rest.astype(BF)
    third = (rest - second.astype(F32)).astype(BF)
    return first, second, third


def iota(shape, axis):
    return lax.broadcasted_iota(jnp.int32, shape, axis)


def history_kernel(lengths, q_ref, k_ref, v_ref, o_ref, m_ref, l_ref, *, per_step, hist, kv, group):
    step = pl.program_id(0)
    heads = kv * group
    for i in range(per_step):
        length = lengths[step * per_step + i]
        q = q_ref[i]
        row_kv = iota((heads, HD), 0) // group
        wide = jnp.concatenate([jnp.where(row_kv == g, q, jnp.zeros_like(q)) for g in range(kv)], 1)
        s = dot_nt(wide, k_ref[i * hist : (i + 1) * hist, :])
        s = jnp.where(iota(s.shape, 1) < length, s, -BIG)
        top = jnp.max(s, -1, keepdims=True) * LOG2
        p = jnp.exp2(s * LOG2 - top)
        total = jnp.sum(p, -1, keepdims=True)
        r = dot_nn(p.astype(BF), v_ref[i * hist : (i + 1) * hist, :])
        o_ref[i] = jnp.concatenate(
            [r[g * group : (g + 1) * group, g * HD : (g + 1) * HD] for g in range(kv)], 0
        )
        m_ref[i] = jnp.broadcast_to(top, (heads, HD))
        l_ref[i] = jnp.broadcast_to(total, (heads, HD))


def history(queries, keys, values, lengths, kv, group):
    rows = queries.shape[0]
    heads = kv * group
    hist = keys.shape[0] // rows
    per_step = math.gcd(rows, 4)
    shape = jax.ShapeDtypeStruct((rows, heads, HD), F32)
    block = pl.BlockSpec((per_step, heads, HD), lambda i, n: (i, 0, 0))
    wide = pl.BlockSpec((per_step * hist, kv * HD), lambda i, n: (i, 0))
    out = pl.pallas_call(
        functools.partial(history_kernel, per_step=per_step, hist=hist, kv=kv, group=group),
        grid_spec=pltpu.PrefetchScalarGridSpec(
            num_scalar_prefetch=1,
            grid=(rows // per_step,),
            in_specs=[block, wide, wide],
            out_specs=[block] * 3,
        ),
        out_shape=[shape] * 3,
        cost_estimate=pl.CostEstimate(
            flops=4 * rows * heads * hist * HD * kv, bytes_accessed=4 * keys.size, transcendentals=0
        ),
        name="history",
    )(lengths, queries.reshape(rows, heads, HD), keys, values)
    return [x.reshape(rows, heads * HD) for x in out]


def prefix_kernel(*refs, sources, rows, kv, group):
    me_ref, task_col, task_row = refs[:3]
    pieces = refs[3 : 3 + sources]
    ck, cv, tk, tv = refs[3 + sources : 7 + sources]
    outs = refs[7 + sources : 7 + 2 * sources]
    q_all, qs, s_ref, vtc, vtt, acc_ref, m_ref, pay = refs[7 + 2 * sources :]
    me = me_ref[0]
    my_task = me // HOLDERS
    heads = kv * group
    lanes = heads * HD
    everyone = sources * rows
    part = COLS // group
    blocks = everyone // part

    for source, target in ((cv, vtc), (tv, vtt)):
        for g in range(kv):
            for c in range(source.shape[0] // STEP):
                target[g, :HD, c * STEP : (c + 1) * STEP] = source[
                    c * STEP : (c + 1) * STEP, g * HD : (g + 1) * HD
                ].T
            target[g, HD:, :] = jnp.ones((AUG - HD, source.shape[0]), BF)

    def slots(match, tri, axis):
        ones = match.astype(BF)
        count = dot_nn(ones, tri) if axis else dot_nn(tri, ones)
        number = iota(count.shape, axis).astype(F32)
        live = jnp.sum(match.astype(F32), axis, keepdims=True)
        return jnp.where(match, count - 1.0, live + number - count).astype(jnp.int32)

    square = (everyone, everyone)
    row_match = jnp.broadcast_to(task_row[...], (8, everyone)) == my_task
    upper = (iota(square, 0) <= iota(square, 1)).astype(BF)
    slot_row = slots(row_match, upper, 1)[:1]
    col_match = jnp.broadcast_to(task_col[...], square) == my_task
    lower = (iota(square, 1) <= iota(square, 0)).astype(BF)
    slot_col = slots(col_match, lower, 0)
    to_sorted = (iota(square, 0) == slot_row).astype(BF)
    from_sorted = (iota(square, 1) == slot_col).astype(BF)
    matched = jnp.sum((task_row[...] == my_task).astype(jnp.int32))
    task_blocks = (matched + part - 1) // part

    for j in range(sources):
        q_all[pl.ds(pl.multiple_of((me ^ j) * rows, rows), rows), :] = pieces[j][...]
    for g in range(kv):
        for h in range(group):
            at = (g * group + h) * HD
            if h % 2 == 0:
                both = dot_nn(to_sorted, q_all[:, at : at + 2 * HD]) * LOG2
            x = both[:, (h % 2) * HD : (h % 2 + 1) * HD]
            high = x.astype(BF)
            low = (x - high.astype(F32)).astype(BF)
            for b in range(blocks):
                qs[g * blocks + b, h * part : (h + 1) * part, :HD] = high[b * part : (b + 1) * part]
                qs[g * blocks + b, h * part : (h + 1) * part, HD:] = low[b * part : (b + 1) * part]

    def lane(g):
        return pl.ds(pl.multiple_of(g * HD, HD), HD)

    def scores(keys, start, g, index):
        k = keys[start : start + SUB, lane(g)]
        return dot_nt(jnp.concatenate([k, k], 1), qs[index])

    def fold(x, m8):
        x = jnp.max(x.reshape(-1, 8, COLS), 0)
        return x if m8 is None else jnp.maximum(m8, x)

    def stages(keys, vt, where_of, first_state, finish, count):
        n = keys.shape[0] // STEP

        def head(index, slot):
            b, g = where_of(index)
            m8 = None
            for c in range(0, STEP, SUB):
                s = scores(keys, c, g, b)
                s_ref[slot, c : c + SUB] = s
                m8 = fold(s, m8)
            return m8

        def body(i, m8):
            b, g = where_of(i)
            b_next, g_next = where_of(jnp.minimum(i + 1, count - 1))
            m, acc, valid = first_state(b)
            for stage in range(n):
                now, later = stage % 2, (stage + 1) % 2
                top = jnp.max(m8, 0, keepdims=True)
                new = top if m is None else jnp.maximum(m, top)
                if valid is not None:
                    new = jnp.where(valid, new, m)
                    shift = jnp.where(valid, new, BIG)
                else:
                    shift = new
                m8 = None
                r = None
                for c in range(0, STEP, SUB):
                    if stage + 1 < n:
                        s = scores(keys, (stage + 1) * STEP + c, g, b)
                    else:
                        s = scores(keys, c, g_next, b_next)
                    s_ref[later, c : c + SUB] = s
                    m8 = fold(s, m8)
                    p = jnp.exp2(s_ref[now, c : c + SUB] - shift).astype(BF)
                    at = stage * STEP + c
                    y = dot_nn(vt[g, :, at : at + SUB], p)
                    r = y if r is None else r + y
                acc = r if acc is None else acc * jnp.exp2(m - new) + r
                m = new
            finish(b, m, acc)
            return m8

        lax.fori_loop(0, count, body, head(0, 0))

    def keep(b, m, acc):
        acc_ref[b] = acc
        m_ref[b] = jnp.broadcast_to(m, (8, COLS))

    stages(ck, vtc, lambda i: (i, i // blocks), lambda b: (None, None, None), keep, kv * blocks)

    some = jnp.maximum(task_blocks, 1)

    def task_where(i):
        g = i // some
        return g * blocks + (i - g * some), g

    def task_state(b):
        request = lax.rem(b, blocks) * part + lax.rem(iota((1, COLS), 1), part)
        return m_ref[b][:1], acc_ref[b], request < matched

    @pl.when(task_blocks > 0)
    def _():
        stages(tk, vtt, task_where, task_state, keep, kv * task_blocks)

    pay[:, lanes:] = jnp.zeros((everyone, HD), BF)

    def emit(b, _):
        g = b // blocks
        at = pl.ds(pl.multiple_of(lax.rem(b, blocks) * part, part), part)
        acc = acc_ref[b]
        turned = acc[:HD].T.astype(BF)
        both = [x.astype(F32) for x in split3(m_ref[b][:1]) + split3(acc[HD : HD + 1])]
        stats = jnp.concatenate(both + [jnp.zeros((2, COLS), F32)], 0)
        stats = jnp.concatenate([stats] * (HD // 8), 0).T
        place = pay[at, lanes:].astype(F32)
        lane_head = iota((part, HD), 1) // 8
        for h in range(group):
            head = g * group + h
            pay[at, pl.ds(pl.multiple_of(head * HD, HD), HD)] = turned[h * part : (h + 1) * part]
            place = jnp.where(lane_head == head, stats[h * part : (h + 1) * part], place)
        pay[at, lanes:] = place.astype(BF)
        return 0

    lax.fori_loop(0, kv * blocks, emit, 0)
    for c in range(0, lanes + HD, 2 * HD):
        end = min(c + 2 * HD, lanes + HD)
        pay[:, c:end] = dot_nn(from_sorted, pay[:, c:end]).astype(BF)
    for j in range(sources):
        outs[j][...] = pay[pl.ds(pl.multiple_of((me ^ j) * rows, rows), rows), :]


def prefix(me, task_of, pieces, ck, cv, tk, tv, kv, group):
    sources = len(pieces)
    rows, lanes = pieces[0].shape
    everyone = sources * rows
    blocks = everyone * group // COLS
    vmem = pl.BlockSpec(memory_space=pltpu.VMEM)
    return pl.pallas_call(
        functools.partial(prefix_kernel, sources=sources, rows=rows, kv=kv, group=group),
        in_specs=[pl.BlockSpec(memory_space=pltpu.SMEM)] + [vmem] * (6 + sources),
        out_specs=[vmem] * sources,
        out_shape=[jax.ShapeDtypeStruct((rows, lanes + HD), BF)] * sources,
        scratch_shapes=[
            pltpu.VMEM((everyone, lanes), BF),
            pltpu.VMEM((kv * blocks, COLS, 2 * HD), BF),
            pltpu.VMEM((2, STEP, COLS), F32),
            pltpu.VMEM((kv, AUG, cv.shape[0]), BF),
            pltpu.VMEM((kv, AUG, tv.shape[0]), BF),
            pltpu.VMEM((kv * blocks, AUG, COLS), F32),
            pltpu.VMEM((kv * blocks, 8, COLS), F32),
            pltpu.VMEM((everyone, lanes + HD), BF),
        ],
        compiler_params=pltpu.CompilerParams(vmem_limit_bytes=40 * 2**20),
        name="prefix",
    )(me, task_of[:, None], task_of[None, :], *pieces, ck, cv, tk, tv)


def combine_kernel(*refs, sources):
    parts = refs[:sources]
    ho, hm, hl, out = refs[sources:]
    lanes = out.shape[1]
    row, col = iota((HD, lanes), 0), iota((HD, lanes), 1)
    same = row // 8 == col // HD
    take_m = (same & (row % 8 < 3)).astype(BF)
    take_l = (same & (row % 8 >= 3) & (row % 8 < 6)).astype(BF)
    tops = [dot_nn(x[:, lanes:], take_m) for x in parts]
    sums = [dot_nn(x[:, lanes:], take_l) for x in parts]
    peak = hm[...]
    for top in tops:
        peak = jnp.maximum(peak, top)
    factor = jnp.exp2(hm[...] - peak)
    num = ho[...] * factor
    den = hl[...] * factor
    for x, top, total in zip(parts, tops, sums):
        factor = jnp.exp2(top - peak)
        num = num + x[:, :lanes].astype(F32) * factor
        den = den + total * factor
    out[...] = (num / den).astype(BF)


def combine(parts, hist):
    rows, lanes = hist[0].shape
    return pl.pallas_call(
        functools.partial(combine_kernel, sources=len(parts)),
        out_shape=jax.ShapeDtypeStruct((rows, lanes), BF),
        name="combine",
    )(*parts, *hist)


def project_kernel(block, x_ref, w_ref, o_ref, acc):
    step = pl.program_id(0)
    part = dot_nn(x_ref[...], w_ref[...])

    @pl.when(step == 0)
    def _():
        acc[...] = part

    @pl.when(step > 0)
    def _():
        acc[...] += part

    @pl.when(step == pl.num_programs(0) - 1)
    def _():
        o_ref[...] = acc[...].astype(o_ref.dtype)


def project(x, w, block, columns, dtype):
    rows, depth = x.shape
    steps = 4
    tall = depth // steps
    return pl.pallas_call(
        project_kernel,
        grid_spec=pltpu.PrefetchScalarGridSpec(
            num_scalar_prefetch=1,
            grid=(steps,),
            in_specs=[
                pl.BlockSpec((rows, tall), lambda i, b: (0, i)),
                pl.BlockSpec((tall, columns), lambda i, b: (i, b[0])),
            ],
            out_specs=pl.BlockSpec((rows, columns), lambda i, b: (0, 0)),
            scratch_shapes=[pltpu.VMEM((rows, columns), F32)],
        ),
        out_shape=jax.ShapeDtypeStruct((rows, columns), dtype),
        cost_estimate=pl.CostEstimate(
            flops=2 * rows * depth * columns, bytes_accessed=2 * depth * columns, transcendentals=0
        ),
        name="project",
    )(block, x, w)


def shards(
    queries,
    corpus_keys,
    corpus_values,
    task_keys,
    task_values,
    history_keys,
    history_values,
    history_lengths,
    task_of,
    out_weight,
):
    kv = corpus_keys.shape[1] // HD
    group = queries.shape[1] // HD // kv
    nreq, nkvh = lax.axis_size("req"), lax.axis_size("kvh")
    me_req, me_kvh = lax.axis_index("req"), lax.axis_index("kvh")

    def swap(x, axis, size, bit):
        return lax.ppermute(x, axis, [(i, i ^ bit) for i in range(size)])

    pieces = [None] * nreq
    pieces[0] = queries
    for bit in range(nreq - 2, 1, -2):
        pieces[bit] = swap(queries, "req", nreq, bit)
    for bit in range(0, nreq, 2):
        pieces[bit + 1] = swap(pieces[bit], "req", nreq, 1)

    hist = history(queries, history_keys, history_values, history_lengths, kv, group)

    me = me_req.astype(jnp.int32).reshape(1)
    parts = prefix(
        me, task_of, pieces, corpus_keys, corpus_values, task_keys, task_values, kv, group
    )
    parts = list(parts[:1]) + [swap(parts[j], "req", nreq, j) for j in range(1, nreq)]
    attended = combine(parts, hist)

    columns = out_weight.shape[1] // nkvh
    total = None
    came = []
    for bit in list(range(nkvh - 1, 0, -1)) + [0]:
        block = (me_kvh ^ bit).astype(jnp.int32).reshape(1)
        y = project(attended, out_weight, block, columns, BF if bit else F32)
        if bit:
            came.append(swap(y, "kvh", nkvh, bit))
        else:
            total = y
    for y in came:
        total = total + y.astype(F32)
    return total.astype(BF)


def solution(mesh):
    return jax.shard_map(
        shards,
        mesh=mesh,
        in_specs=(
            P("req", "kvh"),
            P("req", "kvh"),
            P("req", "kvh"),
            P("req", "kvh"),
            P("req", "kvh"),
            P("req", "kvh"),
            P("req", "kvh"),
            P("req"),
            P(),
            P("kvh", None),
        ),
        out_specs=P("req", "kvh"),
        check_vma=False,
    )
```

```python
import functools
import math

import jax
import jax.numpy as jnp
from jax import lax
from jax.experimental import pallas as pl
from jax.experimental.pallas import tpu as pltpu
from jax.sharding import PartitionSpec as P

HD = 128
HOLDERS = 2
LOG2 = math.log2(math.e) / math.sqrt(HD)
BIG = 1e30
COLS = 256
STEP = 1024
SUB = 512
CHUNKS = 8
AUG = 144
BF = jnp.bfloat16
F32 = jnp.float32


def dot_nt(a, b):
    return lax.dot_general(a, b, (((1,), (1,)), ((), ())), preferred_element_type=F32)


def dot_nn(a, b):
    return lax.dot_general(a, b, (((1,), (0,)), ((), ())), preferred_element_type=F32)


def split3(x):
    first = x.astype(BF)
    rest = x - first.astype(F32)
    second = rest.astype(BF)
    third = (rest - second.astype(F32)).astype(BF)
    return first, second, third


def iota(shape, axis):
    return lax.broadcasted_iota(jnp.int32, shape, axis)


def history_kernel(
    lengths, q_ref, k_any, v_any, c_any, t_any, o_ref, m_ref, l_ref, vtc, vtt,
    q32, kbuf, vbuf, cbuf, tbuf, sems, *, waves, hist, kv, group
):
    heads = kv * group
    rows = q_ref.shape[0]
    per = rows // waves
    tall = per * hist
    copies = []
    for w in range(waves):
        at = slice(w * tall, (w + 1) * tall)
        copies.append(
            [
                pltpu.make_async_copy(src.at[at], dst.at[at], sems.at[n, w])
                for n, (src, dst) in enumerate(((k_any, kbuf), (v_any, vbuf)))
            ]
        )
    turns = [
        pltpu.make_async_copy(src, dst, sems.at[n, waves])
        for n, (src, dst) in enumerate(((c_any, cbuf), (t_any, tbuf)))
    ]
    for pair in copies + [turns]:
        for copy in pair:
            copy.start()
    q32[...] = q_ref[...].astype(F32)
    row = iota((heads, HD), 0)
    for w in range(waves):
        for copy in copies[w]:
            copy.wait()
        ids = range(w * per, (w + 1) * per)
        scored = []
        for i in ids:
            wide = []
            for g in range(kv):
                q = jnp.zeros((heads, HD), F32)
                for h in range(g * group, (g + 1) * group):
                    line = q32[i : i + 1, h * HD : (h + 1) * HD]
                    q = jnp.where(row == h, jnp.broadcast_to(line, (heads, HD)), q)
                wide.append(q.astype(BF))
            s = dot_nt(jnp.concatenate(wide, 1), kbuf[i * hist : (i + 1) * hist, :])
            scored.append(jnp.where(iota(s.shape, 1) < lengths[i], s, -BIG))
        tops = [jnp.max(s, -1, keepdims=True) * LOG2 for s in scored]
        ps = [jnp.exp2(s * LOG2 - top) for s, top in zip(scored, tops)]
        totals = [jnp.sum(p, -1, keepdims=True) for p in ps]
        for i, p, top, total in zip(ids, ps, tops, totals):
            r = dot_nn(p.astype(BF), vbuf[i * hist : (i + 1) * hist, :])
            top = jnp.broadcast_to(top, (heads, HD))
            total = jnp.broadcast_to(total, (heads, HD))
            for h in range(heads):
                g = h // group
                to = slice(h * HD, (h + 1) * HD)
                o_ref[i : i + 1, to] = r[h : h + 1, g * HD : (g + 1) * HD]
                m_ref[i : i + 1, to] = top[h : h + 1]
                l_ref[i : i + 1, to] = total[h : h + 1]
    for copy, source, target in zip(turns, (cbuf, tbuf), (vtc, vtt)):
        copy.wait()
        for g in range(kv):
            for c in range(0, source.shape[0], STEP):
                target[g, :HD, c : c + STEP] = source[c : c + STEP, g * HD : (g + 1) * HD].T
            target[g, HD:, :] = jnp.ones((AUG - HD, source.shape[0]), BF)


def history(queries, keys, values, lengths, cv, tv, kv, group):
    rows, lanes = queries.shape
    hist = keys.shape[0] // rows
    waves = rows // math.gcd(rows, 4)
    shape = jax.ShapeDtypeStruct((rows, lanes), F32)
    vmem = pl.BlockSpec(memory_space=pltpu.VMEM)
    return pl.pallas_call(
        functools.partial(history_kernel, waves=waves, hist=hist, kv=kv, group=group),
        in_specs=[pl.BlockSpec(memory_space=pltpu.SMEM), vmem]
        + [pl.BlockSpec(memory_space=pltpu.HBM)] * 4,
        out_specs=[vmem] * 5,
        scratch_shapes=[pltpu.VMEM((rows, lanes), F32)]
        + [pltpu.VMEM(x.shape, BF) for x in (keys, values, cv, tv)]
        + [pltpu.SemaphoreType.DMA((2, waves + 1))],
        out_shape=[shape] * 3
        + [jax.ShapeDtypeStruct((kv, AUG, x.shape[0]), BF) for x in (cv, tv)],
        compiler_params=pltpu.CompilerParams(vmem_limit_bytes=58 * 2**20),
        cost_estimate=pl.CostEstimate(
            flops=4 * rows * lanes * hist * kv, bytes_accessed=4 * keys.size, transcendentals=0
        ),
        name="history",
    )(lengths, queries, keys, values, cv, tv)


def prefix_kernel(*refs, sources, rows, kv, group):
    task_row = refs[0]
    pieces = refs[1 : 1 + sources]
    ck, vtc, tk, vtt, weight = refs[1 + sources : 6 + sources]
    own_out, sent_out = refs[6 + sources : 8 + sources]
    kept = refs[8 + sources : 8 + sources + CHUNKS]
    q_all, qs, s_ref, acc_ref, m_ref, pay, sems = refs[8 + sources + CHUNKS :]
    tall = weight.shape[0] // CHUNKS
    fetches = [
        pltpu.make_async_copy(
            weight.at[i * tall : (i + 1) * tall], kept[i], sems.at[i]
        )
        for i in range(CHUNKS)
    ]
    for fetch in fetches:
        fetch.start()
    me = lax.axis_index("req")
    my_task = me // HOLDERS
    heads = kv * group
    lanes = heads * HD
    everyone = sources * rows
    part = COLS // group
    blocks = everyone // part

    square = (everyone, everyone)
    match = jnp.broadcast_to(task_row[...], (8, everyone)) == my_task
    count = dot_nn(match.astype(BF), (iota(square, 0) <= iota(square, 1)).astype(BF))
    live = jnp.sum(match.astype(F32), 1, keepdims=True)
    slot = jnp.where(match, count - 1.0, live + iota(count.shape, 1).astype(F32) - count)
    hot = (iota(square, 0) == slot[:1].astype(jnp.int32)).astype(F32)
    to_sorted = hot.astype(BF)
    from_sorted = hot.T.astype(BF)
    matched = jnp.sum((task_row[...] == my_task).astype(jnp.int32))
    task_blocks = (matched + part - 1) // part

    for j in range(sources):
        q_all[pl.ds(pl.multiple_of((me ^ j) * rows, rows), rows), :] = pieces[j][...]
    for g in range(kv):
        for h in range(group):
            at = (g * group + h) * HD
            if h % 2 == 0:
                both = dot_nn(to_sorted, q_all[:, at : at + 2 * HD]) * LOG2
            x = both[:, (h % 2) * HD : (h % 2 + 1) * HD]
            high = x.astype(BF)
            low = (x - high.astype(F32)).astype(BF)
            for b in range(blocks):
                qs[g * blocks + b, h * part : (h + 1) * part, :HD] = high[b * part : (b + 1) * part]
                qs[g * blocks + b, h * part : (h + 1) * part, HD:] = low[b * part : (b + 1) * part]

    def lane(g):
        return pl.ds(pl.multiple_of(g * HD, HD), HD)

    def scores(keys, start, g, index):
        k = keys[start : start + SUB, lane(g)]
        return dot_nt(jnp.concatenate([k, k], 1), qs[index])

    def fold(x, m8):
        x = jnp.max(x.reshape(-1, 8, COLS), 0)
        return x if m8 is None else jnp.maximum(m8, x)

    def stages(keys, vt, where_of, first_state, finish, count):
        n = keys.shape[0] // STEP

        def head(index, slot):
            b, g = where_of(index)
            m8 = None
            for c in range(0, STEP, SUB):
                s = scores(keys, c, g, b)
                s_ref[slot, c : c + SUB] = s
                m8 = fold(s, m8)
            return m8

        def body(i, m8):
            b, g = where_of(i)
            b_next, g_next = where_of(jnp.minimum(i + 1, count - 1))
            m, acc, valid = first_state(b)
            for stage in range(n):
                now, later = stage % 2, (stage + 1) % 2
                top = jnp.max(m8, 0, keepdims=True)
                new = top if m is None else jnp.maximum(m, top)
                if valid is not None:
                    new = jnp.where(valid, new, m)
                    shift = jnp.where(valid, new, BIG)
                else:
                    shift = new
                m8 = None
                r = None
                for c in range(0, STEP, SUB):
                    if stage + 1 < n:
                        s = scores(keys, (stage + 1) * STEP + c, g, b)
                    else:
                        s = scores(keys, c, g_next, b_next)
                    s_ref[later, c : c + SUB] = s
                    m8 = fold(s, m8)
                    p = jnp.exp2(s_ref[now, c : c + SUB] - shift).astype(BF)
                    at = stage * STEP + c
                    y = dot_nn(vt[g, :, at : at + SUB], p)
                    r = y if r is None else r + y
                acc = r if acc is None else acc * jnp.exp2(m - new) + r
                m = new
            finish(b, m, acc)
            return m8

        lax.fori_loop(0, count, body, head(0, 0))

    def keep(b, m, acc):
        acc_ref[b] = acc
        m_ref[b] = jnp.broadcast_to(m, (8, COLS))

    stages(ck, vtc, lambda i: (i, i // blocks), lambda b: (None, None, None), keep, kv * blocks)

    some = jnp.maximum(task_blocks, 1)

    def task_where(i):
        g = i // some
        return g * blocks + (i - g * some), g

    def task_state(b):
        request = lax.rem(b, blocks) * part + lax.rem(iota((1, COLS), 1), part)
        return m_ref[b][:1], acc_ref[b], request < matched

    @pl.when(task_blocks > 0)
    def _():
        stages(tk, vtt, task_where, task_state, keep, kv * task_blocks)

    pay[:, lanes:] = jnp.zeros((everyone, HD), BF)

    def emit(b, _):
        g = b // blocks
        at = pl.ds(pl.multiple_of(lax.rem(b, blocks) * part, part), part)
        acc = acc_ref[b]
        turned = acc[:HD].T.astype(BF)
        both = [x.astype(F32) for x in split3(m_ref[b][:1]) + split3(acc[HD : HD + 1])]
        stats = jnp.concatenate(both + [jnp.zeros((2, COLS), F32)], 0)
        stats = jnp.concatenate([stats] * (HD // 8), 0).T
        place = pay[at, lanes:].astype(F32)
        lane_head = iota((part, HD), 1) // 8
        for h in range(group):
            head = g * group + h
            pay[at, pl.ds(pl.multiple_of(head * HD, HD), HD)] = turned[h * part : (h + 1) * part]
            place = jnp.where(lane_head == head, stats[h * part : (h + 1) * part], place)
        pay[at, lanes:] = place.astype(BF)
        return 0

    lax.fori_loop(0, kv * blocks, emit, 0)
    for c in range(0, lanes + HD, 2 * HD):
        end = min(c + 2 * HD, lanes + HD)
        pay[:, c:end] = dot_nn(from_sorted, pay[:, c:end]).astype(BF)
    for j in range(sources):
        out = sent_out if j % 2 else own_out
        out[j // 2 * rows : (j // 2 + 1) * rows, :] = pay[
            pl.ds(pl.multiple_of((me ^ j) * rows, rows), rows), :
        ]
    for fetch in fetches:
        fetch.wait()


def prefix(task_of, pieces, ck, vtc, tk, vtt, weight, kv, group):
    sources = len(pieces)
    rows, lanes = pieces[0].shape
    everyone = sources * rows
    blocks = everyone * group // COLS
    vmem = pl.BlockSpec(memory_space=pltpu.VMEM)
    return pl.pallas_call(
        functools.partial(prefix_kernel, sources=sources, rows=rows, kv=kv, group=group),
        in_specs=[vmem] * (5 + sources) + [pl.BlockSpec(memory_space=pltpu.HBM)],
        out_specs=[vmem] * (2 + CHUNKS),
        out_shape=[jax.ShapeDtypeStruct((everyone // 2, lanes + HD), BF)] * 2
        + [pltpu.VMEM((weight.shape[0] // CHUNKS, weight.shape[1]), BF)] * CHUNKS,
        scratch_shapes=[
            pltpu.VMEM((everyone, lanes), BF),
            pltpu.VMEM((kv * blocks, COLS, 2 * HD), BF),
            pltpu.VMEM((2, STEP, COLS), F32),
            pltpu.VMEM((kv * blocks, AUG, COLS), F32),
            pltpu.VMEM((kv * blocks, 8, COLS), F32),
            pltpu.VMEM((everyone, lanes + HD), BF),
            pltpu.SemaphoreType.DMA((CHUNKS,)),
        ],
        compiler_params=pltpu.CompilerParams(vmem_limit_bytes=7 * 2**20),
        name="prefix",
    )(task_of[None, :], *pieces, ck, vtc, tk, vtt, weight)


def merge_kernel(a_ref, b_ref, *outs):
    rows, wide = a_ref.shape
    lanes = wide - HD
    part = rows // len(outs)
    row, col = iota((HD, HD), 0), iota((HD, HD), 1)
    same = row // 8 == col // 8
    take_m = (same & (row % 8 < 3)).astype(BF)
    take_l = (same & (row % 8 >= 3) & (row % 8 < 6)).astype(BF)
    spread = (iota((2 * HD, lanes), 0) % HD == iota((2 * HD, lanes), 1) // HD * 8).astype(BF)
    sa, sb = a_ref[:, lanes:], b_ref[:, lanes:]
    ma, mb = dot_nn(sa, take_m), dot_nn(sb, take_m)
    peak = jnp.maximum(ma, mb)
    fa, fb = jnp.exp2(ma - peak), jnp.exp2(mb - peak)
    total = dot_nn(sa, take_l) * fa + dot_nn(sb, take_l) * fb

    def widen(x):
        high = x.astype(BF)
        low = (x - high.astype(F32)).astype(BF)
        return dot_nn(jnp.concatenate([high, low], 1), spread)

    out = a_ref[:, :lanes].astype(F32) * widen(fa) + b_ref[:, :lanes].astype(F32) * widen(fb)
    out = out.astype(BF)
    place = iota(peak.shape, 1) % 8
    stats = jnp.zeros(peak.shape, F32)
    for i, x in enumerate(split3(peak) + split3(total)):
        stats = jnp.where(place == i, x.astype(F32), stats)
    stats = stats.astype(BF)
    for j, ref in enumerate(outs):
        ref[:, :lanes] = out[j * part : (j + 1) * part]
        ref[:, lanes:] = stats[j * part : (j + 1) * part]


def merge(a, b, pieces):
    shape = jax.ShapeDtypeStruct((a.shape[0] // pieces, a.shape[1]), BF)
    vmem = pl.BlockSpec(memory_space=pltpu.VMEM)
    return pl.pallas_call(
        merge_kernel,
        in_specs=[vmem] * 2,
        out_specs=[vmem] * pieces,
        out_shape=[shape] * pieces,
        compiler_params=pltpu.CompilerParams(vmem_limit_bytes=3 * 2**20),
        name="merge",
    )(a, b)


def product(bit, x, w_refs, o_ref):
    columns = o_ref.shape[1]
    at = pl.ds(pl.multiple_of((lax.axis_index("kvh") ^ bit) * columns, columns), columns)
    y = None
    for i, w_ref in enumerate(w_refs):
        tall = w_ref.shape[0]
        part = dot_nn(x[:, i * tall : (i + 1) * tall], w_ref[:, at])
        y = part if y is None else y + part
    o_ref[...] = y.astype(o_ref.dtype)


def combine_kernel(*refs, sources, bit):
    parts = refs[:sources]
    ho, hm, hl = refs[sources : sources + 3]
    w_refs = refs[sources + 3 : -2]
    out, y_ref = refs[-2:]
    lanes = out.shape[1]
    row, col = iota((HD, lanes), 0), iota((HD, lanes), 1)
    same = row // 8 == col // HD
    take_m = (same & (row % 8 < 3)).astype(BF)
    take_l = (same & (row % 8 >= 3) & (row % 8 < 6)).astype(BF)
    tops = [dot_nn(x[:, lanes:], take_m) for x in parts]
    sums = [dot_nn(x[:, lanes:], take_l) for x in parts]
    peak = hm[...]
    for top in tops:
        peak = jnp.maximum(peak, top)
    factor = jnp.exp2(hm[...] - peak)
    num = ho[...] * factor
    den = hl[...] * factor
    for x, top, total in zip(parts, tops, sums):
        factor = jnp.exp2(top - peak)
        num = num + x[:, :lanes].astype(F32) * factor
        den = den + total * factor
    attended = (num / den).astype(BF)
    out[...] = attended
    product(bit, attended, w_refs, y_ref)


def project_kernel(x_ref, *refs, bit):
    product(bit, x_ref[...], refs[:-1], refs[-1])


def with_weight(kernel, name, operands, weight, shapes):
    vmem = pl.BlockSpec(memory_space=pltpu.VMEM)
    out = pl.pallas_call(
        kernel,
        in_specs=[vmem] * (len(operands) + len(weight)),
        out_specs=[vmem] * len(shapes),
        out_shape=shapes,
        compiler_params=pltpu.CompilerParams(vmem_limit_bytes=2 * 2**20),
        name=name,
    )(*operands, *weight)
    return out


def shards(
    queries,
    corpus_keys,
    corpus_values,
    task_keys,
    task_values,
    history_keys,
    history_values,
    history_lengths,
    task_of,
    out_weight,
):
    kv = corpus_keys.shape[1] // HD
    group = queries.shape[1] // HD // kv
    nreq, nkvh = lax.axis_size("req"), lax.axis_size("kvh")

    def swap(x, axis, size, bit):
        return lax.ppermute(x, axis, [(i, i ^ bit) for i in range(size)])

    pieces = [None] * nreq
    pieces[0] = queries
    for bit in range(nreq - 2, 1, -2):
        pieces[bit] = swap(queries, "req", nreq, bit)
    pieces[1] = swap(queries, "req", nreq, 1)

    *hist, vtc, vtt = history(
        queries, history_keys, history_values, history_lengths, corpus_values, task_values, kv, group
    )
    across = [pieces[bit] for bit in range(2, nreq, 2)]
    across, hist, vtc, vtt = lax.optimization_barrier((across, hist, vtc, vtt))
    for i, piece in enumerate(across):
        pieces[2 * i + 2] = piece
        pieces[2 * i + 3] = swap(piece, "req", nreq, 1)

    own, sent, *weight = prefix(
        task_of, pieces, corpus_keys, vtc, task_keys, vtt, out_weight, kv, group
    )
    parts = list(merge(own, swap(sent, "req", nreq, 1), nreq // 2))
    for j in range(nreq // 2 - 1, 0, -1):
        parts[j] = swap(parts[j], "req", nreq, 2 * j)

    rows = queries.shape[0]
    columns = out_weight.shape[1] // nkvh
    attended = None
    came = []
    for bit in list(range(nkvh - 1, 0, -1)) + [0]:
        shape = jax.ShapeDtypeStruct((rows, columns), BF if bit else F32)
        if attended is None:
            attended, y = with_weight(
                functools.partial(combine_kernel, sources=len(parts), bit=bit),
                "combine",
                parts + list(hist),
                weight,
                [jax.ShapeDtypeStruct(queries.shape, BF), shape],
            )
        else:
            kernel = functools.partial(project_kernel, bit=bit)
            (y,) = with_weight(kernel, "project", [attended], weight, [shape])
        came.append(swap(y, "kvh", nkvh, bit) if bit else y)
    total = came[-1]
    for y in came[:-1]:
        total = total + y.astype(F32)
    return total.astype(BF)


def solution(mesh):
    return jax.shard_map(
        shards,
        mesh=mesh,
        in_specs=(
            P("req", "kvh"),
            P("req", "kvh"),
            P("req", "kvh"),
            P("req", "kvh"),
            P("req", "kvh"),
            P("req", "kvh"),
            P("req", "kvh"),
            P("req"),
            P(),
            P("kvh", None),
        ),
        out_specs=P("req", "kvh"),
        check_vma=False,
    )
```

```python
import functools
import math

import jax
import jax.numpy as jnp
from jax import lax
from jax.experimental import pallas as pl
from jax.experimental.pallas import tpu as pltpu
from jax.sharding import PartitionSpec as P


HD = 128
HOLDERS = 2
LOG2 = math.log2(math.e) / math.sqrt(HD)
BIG = 1e30
COLS = 256
STEP = 1024
SUB = 512
CHUNKS = 8
AUG = 144
BF = jnp.bfloat16
F32 = jnp.float32


def dot_nt(a, b):
    return lax.dot_general(a, b, (((1,), (1,)), ((), ())), preferred_element_type=F32)


def dot_nn(a, b):
    return lax.dot_general(a, b, (((1,), (0,)), ((), ())), preferred_element_type=F32)


def split3(x):
    first = x.astype(BF)
    rest = x - first.astype(F32)
    second = rest.astype(BF)
    third = (rest - second.astype(F32)).astype(BF)
    return first, second, third


def iota(shape, axis):
    return lax.broadcasted_iota(jnp.int32, shape, axis)


def history_kernel(
    lengths, q_ref, k_any, v_any, c_any, t_any, o_ref, m_ref, l_ref, vtc, vtt,
    q32, kbuf, vbuf, cbuf, tbuf, sems, *, waves, hist, kv, group
):
    heads = kv * group
    rows = q_ref.shape[0]
    per = rows // waves
    tall = per * hist
    copies = []
    for w in range(waves):
        at = slice(w * tall, (w + 1) * tall)
        copies.append(
            [
                pltpu.make_async_copy(src.at[at], dst.at[at], sems.at[n, w])
                for n, (src, dst) in enumerate(((k_any, kbuf), (v_any, vbuf)))
            ]
        )
    turns = [
        pltpu.make_async_copy(src, dst, sems.at[n, waves])
        for n, (src, dst) in enumerate(((c_any, cbuf), (t_any, tbuf)))
    ]
    for pair in copies + [turns]:
        for copy in pair:
            copy.start()
    q32[...] = q_ref[...].astype(F32)
    row = iota((heads, HD), 0)
    for w in range(waves):
        for copy in copies[w]:
            copy.wait()
        ids = range(w * per, (w + 1) * per)
        scored = []
        for i in ids:
            wide = []
            for g in range(kv):
                q = jnp.zeros((heads, HD), F32)
                for h in range(g * group, (g + 1) * group):
                    line = q32[i : i + 1, h * HD : (h + 1) * HD]
                    q = jnp.where(row == h, jnp.broadcast_to(line, (heads, HD)), q)
                wide.append(q.astype(BF))
            s = dot_nt(jnp.concatenate(wide, 1), kbuf[i * hist : (i + 1) * hist, :])
            scored.append(jnp.where(iota(s.shape, 1) < lengths[i], s, -BIG))
        tops = [jnp.max(s, -1, keepdims=True) * LOG2 for s in scored]
        ps = [jnp.exp2(s * LOG2 - top) for s, top in zip(scored, tops)]
        totals = [jnp.sum(p, -1, keepdims=True) for p in ps]
        for i, p, top, total in zip(ids, ps, tops, totals):
            r = dot_nn(p.astype(BF), vbuf[i * hist : (i + 1) * hist, :])
            top = jnp.broadcast_to(top, (heads, HD))
            total = jnp.broadcast_to(total, (heads, HD))
            for h in range(heads):
                g = h // group
                to = slice(h * HD, (h + 1) * HD)
                o_ref[i : i + 1, to] = r[h : h + 1, g * HD : (g + 1) * HD]
                m_ref[i : i + 1, to] = top[h : h + 1]
                l_ref[i : i + 1, to] = total[h : h + 1]
    for copy, source, target in zip(turns, (cbuf, tbuf), (vtc, vtt)):
        copy.wait()
        for g in range(kv):
            for c in range(0, source.shape[0], STEP):
                target[g, :HD, c : c + STEP] = source[c : c + STEP, g * HD : (g + 1) * HD].T
            target[g, HD:, :] = jnp.ones((AUG - HD, source.shape[0]), BF)


def history(queries, keys, values, lengths, cv, tv, kv, group):
    rows, lanes = queries.shape
    hist = keys.shape[0] // rows
    waves = rows // math.gcd(rows, 4)
    shape = jax.ShapeDtypeStruct((rows, lanes), F32)
    vmem = pl.BlockSpec(memory_space=pltpu.VMEM)
    return pl.pallas_call(
        functools.partial(history_kernel, waves=waves, hist=hist, kv=kv, group=group),
        in_specs=[pl.BlockSpec(memory_space=pltpu.SMEM), vmem]
        + [pl.BlockSpec(memory_space=pltpu.HBM)] * 4,
        out_specs=[vmem] * 5,
        scratch_shapes=[pltpu.VMEM((rows, lanes), F32)]
        + [pltpu.VMEM(x.shape, BF) for x in (keys, values, cv, tv)]
        + [pltpu.SemaphoreType.DMA((2, waves + 1))],
        out_shape=[shape] * 3
        + [jax.ShapeDtypeStruct((kv, AUG, x.shape[0]), BF) for x in (cv, tv)],
        compiler_params=pltpu.CompilerParams(vmem_limit_bytes=22 * 2**20),
        cost_estimate=pl.CostEstimate(
            flops=4 * rows * lanes * hist * kv, bytes_accessed=4 * keys.size, transcendentals=0
        ),
        name="history",
    )(lengths, queries, *[pltpu.with_memory_space_constraint(x, pltpu.HBM) for x in (keys, values, cv, tv)])


def prefix_kernel(*refs, sources, rows, kv, group):
    task_row = refs[0]
    pieces = refs[1 : 1 + sources]
    ck, vtc, tk, vtt, weight = refs[1 + sources : 6 + sources]
    own_out, sent_out = refs[6 + sources : 8 + sources]
    kept = refs[8 + sources : 8 + sources + CHUNKS]
    q_all, qs, s_ref, acc_ref, m_ref, pay, sems = refs[8 + sources + CHUNKS :]
    tall = weight.shape[0] // CHUNKS
    fetches = [
        pltpu.make_async_copy(
            weight.at[i * tall : (i + 1) * tall], kept[i], sems.at[i]
        )
        for i in range(CHUNKS)
    ]
    for fetch in fetches:
        fetch.start()
    me = lax.axis_index("req")
    my_task = me // HOLDERS
    heads = kv * group
    lanes = heads * HD
    everyone = sources * rows
    part = COLS // group
    blocks = everyone // part

    square = (everyone, everyone)
    match = jnp.broadcast_to(task_row[...], (8, everyone)) == my_task
    count = dot_nn(match.astype(BF), (iota(square, 0) <= iota(square, 1)).astype(BF))
    live = jnp.sum(match.astype(F32), 1, keepdims=True)
    slot = jnp.where(match, count - 1.0, live + iota(count.shape, 1).astype(F32) - count)
    hot = (iota(square, 0) == slot[:1].astype(jnp.int32)).astype(F32)
    to_sorted = hot.astype(BF)
    from_sorted = hot.T.astype(BF)
    matched = jnp.sum((task_row[...] == my_task).astype(jnp.int32))
    task_blocks = (matched + part - 1) // part

    for j in range(sources):
        q_all[pl.ds(pl.multiple_of((me ^ j) * rows, rows), rows), :] = pieces[j][...]
    for g in range(kv):
        for h in range(group):
            at = (g * group + h) * HD
            if h % 2 == 0:
                both = dot_nn(to_sorted, q_all[:, at : at + 2 * HD]) * LOG2
            x = both[:, (h % 2) * HD : (h % 2 + 1) * HD]
            high = x.astype(BF)
            low = (x - high.astype(F32)).astype(BF)
            for b in range(blocks):
                qs[g * blocks + b, h * part : (h + 1) * part, :HD] = high[b * part : (b + 1) * part]
                qs[g * blocks + b, h * part : (h + 1) * part, HD:] = low[b * part : (b + 1) * part]

    def lane(g):
        return pl.ds(pl.multiple_of(g * HD, HD), HD)

    def scores(keys, start, g, index):
        k = keys[start : start + SUB, lane(g)]
        return dot_nt(jnp.concatenate([k, k], 1), qs[index])

    def fold(x, m8):
        x = jnp.max(x.reshape(-1, 8, COLS), 0)
        return x if m8 is None else jnp.maximum(m8, x)

    def stages(keys, vt, where_of, first_state, finish, count):
        n = keys.shape[0] // STEP

        def head(index, slot):
            b, g = where_of(index)
            m8 = None
            for c in range(0, STEP, SUB):
                s = scores(keys, c, g, b)
                s_ref[slot, c : c + SUB] = s
                m8 = fold(s, m8)
            return m8

        def body(i, m8):
            b, g = where_of(i)
            b_next, g_next = where_of(jnp.minimum(i + 1, count - 1))
            m, acc, valid = first_state(b)
            for stage in range(n):
                now, later = stage % 2, (stage + 1) % 2
                top = jnp.max(m8, 0, keepdims=True)
                new = top if m is None else jnp.maximum(m, top)
                if valid is not None:
                    new = jnp.where(valid, new, m)
                    shift = jnp.where(valid, new, BIG)
                else:
                    shift = new
                m8 = None
                r = None
                for c in range(0, STEP, SUB):
                    if stage + 1 < n:
                        s = scores(keys, (stage + 1) * STEP + c, g, b)
                    else:
                        s = scores(keys, c, g_next, b_next)
                    s_ref[later, c : c + SUB] = s
                    m8 = fold(s, m8)
                    p = jnp.exp2(s_ref[now, c : c + SUB] - shift).astype(BF)
                    at = stage * STEP + c
                    y = dot_nn(vt[g, :, at : at + SUB], p)
                    r = y if r is None else r + y
                acc = r if acc is None else acc * jnp.exp2(m - new) + r
                m = new
            finish(b, m, acc)
            return m8

        lax.fori_loop(0, count, body, head(0, 0))

    def keep(b, m, acc):
        acc_ref[b] = acc
        m_ref[b] = jnp.broadcast_to(m, (8, COLS))

    stages(ck, vtc, lambda i: (i, i // blocks), lambda b: (None, None, None), keep, kv * blocks)

    some = jnp.maximum(task_blocks, 1)

    def task_where(i):
        g = i // some
        return g * blocks + (i - g * some), g

    def task_state(b):
        request = lax.rem(b, blocks) * part + lax.rem(iota((1, COLS), 1), part)
        return m_ref[b][:1], acc_ref[b], request < matched

    @pl.when(task_blocks > 0)
    def _():
        stages(tk, vtt, task_where, task_state, keep, kv * task_blocks)

    pay[:, lanes:] = jnp.zeros((everyone, HD), BF)

    def emit(b, _):
        g = b // blocks
        at = pl.ds(pl.multiple_of(lax.rem(b, blocks) * part, part), part)
        acc = acc_ref[b]
        turned = acc[:HD].T.astype(BF)
        both = [x.astype(F32) for x in split3(m_ref[b][:1]) + split3(acc[HD : HD + 1])]
        stats = jnp.concatenate(both + [jnp.zeros((2, COLS), F32)], 0)
        stats = jnp.concatenate([stats] * (HD // 8), 0).T
        place = pay[at, lanes:].astype(F32)
        lane_head = iota((part, HD), 1) // 8
        for h in range(group):
            head = g * group + h
            pay[at, pl.ds(pl.multiple_of(head * HD, HD), HD)] = turned[h * part : (h + 1) * part]
            place = jnp.where(lane_head == head, stats[h * part : (h + 1) * part], place)
        pay[at, lanes:] = place.astype(BF)
        return 0

    lax.fori_loop(0, kv * blocks, emit, 0)
    for c in range(0, lanes + HD, 2 * HD):
        end = min(c + 2 * HD, lanes + HD)
        pay[:, c:end] = dot_nn(from_sorted, pay[:, c:end]).astype(BF)
    for j in range(sources):
        out = sent_out if j % 2 else own_out
        out[j // 2 * rows : (j // 2 + 1) * rows, :] = pay[
            pl.ds(pl.multiple_of((me ^ j) * rows, rows), rows), :
        ]
    for fetch in fetches:
        fetch.wait()


def prefix(task_of, pieces, ck, vtc, tk, vtt, weight, kv, group):
    sources = len(pieces)
    rows, lanes = pieces[0].shape
    everyone = sources * rows
    blocks = everyone * group // COLS
    vmem = pl.BlockSpec(memory_space=pltpu.VMEM)
    return pl.pallas_call(
        functools.partial(prefix_kernel, sources=sources, rows=rows, kv=kv, group=group),
        in_specs=[vmem] * (5 + sources) + [pl.BlockSpec(memory_space=pltpu.HBM)],
        out_specs=[vmem] * (2 + CHUNKS),
        out_shape=[jax.ShapeDtypeStruct((everyone // 2, lanes + HD), BF)] * 2
        + [pltpu.VMEM((weight.shape[0] // CHUNKS, weight.shape[1]), BF)] * CHUNKS,
        scratch_shapes=[
            pltpu.VMEM((everyone, lanes), BF),
            pltpu.VMEM((kv * blocks, COLS, 2 * HD), BF),
            pltpu.VMEM((2, STEP, COLS), F32),
            pltpu.VMEM((kv * blocks, AUG, COLS), F32),
            pltpu.VMEM((kv * blocks, 8, COLS), F32),
            pltpu.VMEM((everyone, lanes + HD), BF),
            pltpu.SemaphoreType.DMA((CHUNKS,)),
        ],
        compiler_params=pltpu.CompilerParams(vmem_limit_bytes=7 * 2**20),
        name="prefix",
    )(task_of[None, :], *pieces, ck, vtc, tk, vtt, weight)


def merge_kernel(a_ref, b_ref, *outs):
    rows, wide = a_ref.shape
    lanes = wide - HD
    part = rows // len(outs)
    row, col = iota((HD, HD), 0), iota((HD, HD), 1)
    same = row // 8 == col // 8
    take_m = (same & (row % 8 < 3)).astype(BF)
    take_l = (same & (row % 8 >= 3) & (row % 8 < 6)).astype(BF)
    spread = (iota((2 * HD, lanes), 0) % HD == iota((2 * HD, lanes), 1) // HD * 8).astype(BF)
    sa, sb = a_ref[:, lanes:], b_ref[:, lanes:]
    ma, mb = dot_nn(sa, take_m), dot_nn(sb, take_m)
    peak = jnp.maximum(ma, mb)
    fa, fb = jnp.exp2(ma - peak), jnp.exp2(mb - peak)
    total = dot_nn(sa, take_l) * fa + dot_nn(sb, take_l) * fb

    def widen(x):
        high = x.astype(BF)
        low = (x - high.astype(F32)).astype(BF)
        return dot_nn(jnp.concatenate([high, low], 1), spread)

    out = a_ref[:, :lanes].astype(F32) * widen(fa) + b_ref[:, :lanes].astype(F32) * widen(fb)
    out = out.astype(BF)
    place = iota(peak.shape, 1) % 8
    stats = jnp.zeros(peak.shape, F32)
    for i, x in enumerate(split3(peak) + split3(total)):
        stats = jnp.where(place == i, x.astype(F32), stats)
    stats = stats.astype(BF)
    for j, ref in enumerate(outs):
        ref[:, :lanes] = out[j * part : (j + 1) * part]
        ref[:, lanes:] = stats[j * part : (j + 1) * part]


def merge(a, b, pieces):
    shape = jax.ShapeDtypeStruct((a.shape[0] // pieces, a.shape[1]), BF)
    vmem = pl.BlockSpec(memory_space=pltpu.VMEM)
    return pl.pallas_call(
        merge_kernel,
        in_specs=[vmem] * 2,
        out_specs=[vmem] * pieces,
        out_shape=[shape] * pieces,
        compiler_params=pltpu.CompilerParams(vmem_limit_bytes=3 * 2**20),
        name="merge",
    )(a, b)


def product(bit, x, w_refs, o_ref):
    columns = o_ref.shape[1]
    at = pl.ds(pl.multiple_of((lax.axis_index("kvh") ^ bit) * columns, columns), columns)
    y = None
    for i, w_ref in enumerate(w_refs):
        tall = w_ref.shape[0]
        part = dot_nn(x[:, i * tall : (i + 1) * tall], w_ref[:, at])
        y = part if y is None else y + part
    o_ref[...] = y.astype(o_ref.dtype)


def combine_kernel(*refs, sources, bit):
    parts = refs[:sources]
    ho, hm, hl = refs[sources : sources + 3]
    w_refs = refs[sources + 3 : -2]
    out, y_ref = refs[-2:]
    lanes = out.shape[1]
    row, col = iota((HD, lanes), 0), iota((HD, lanes), 1)
    same = row // 8 == col // HD
    take_m = (same & (row % 8 < 3)).astype(BF)
    take_l = (same & (row % 8 >= 3) & (row % 8 < 6)).astype(BF)
    tops = [dot_nn(x[:, lanes:], take_m) for x in parts]
    sums = [dot_nn(x[:, lanes:], take_l) for x in parts]
    peak = hm[...]
    for top in tops:
        peak = jnp.maximum(peak, top)
    factor = jnp.exp2(hm[...] - peak)
    num = ho[...] * factor
    den = hl[...] * factor
    for x, top, total in zip(parts, tops, sums):
        factor = jnp.exp2(top - peak)
        num = num + x[:, :lanes].astype(F32) * factor
        den = den + total * factor
    attended = (num / den).astype(BF)
    out[...] = attended
    product(bit, attended, w_refs, y_ref)


def project_kernel(x_ref, *refs, bit):
    product(bit, x_ref[...], refs[:-1], refs[-1])


def with_weight(kernel, operands, weight, shapes):
    vmem = pl.BlockSpec(memory_space=pltpu.VMEM)
    out = pl.pallas_call(
        kernel,
        in_specs=[vmem] * (len(operands) + len(weight)),
        out_specs=[vmem] * len(shapes),
        out_shape=shapes,
        compiler_params=pltpu.CompilerParams(vmem_limit_bytes=2 * 2**20),
    )(*operands, *weight)
    return out


def shards(
    queries,
    corpus_keys,
    corpus_values,
    task_keys,
    task_values,
    history_keys,
    history_values,
    history_lengths,
    task_of,
    out_weight,
):
    kv = corpus_keys.shape[1] // HD
    group = queries.shape[1] // HD // kv
    nreq, nkvh = lax.axis_size("req"), lax.axis_size("kvh")

    def swap(x, axis, size, bit):
        return lax.ppermute(x, axis, [(i, i ^ bit) for i in range(size)])

    pieces = [None] * nreq
    pieces[0] = queries
    for bit in range(nreq - 2, 1, -2):
        pieces[bit] = swap(queries, "req", nreq, bit)
    pieces[1] = swap(queries, "req", nreq, 1)

    *hist, vtc, vtt = history(
        queries, history_keys, history_values, history_lengths, corpus_values, task_values, kv, group
    )
    across = [pieces[bit] for bit in range(2, nreq, 2)]
    across, hist, vtc, vtt = lax.optimization_barrier((across, hist, vtc, vtt))
    for i, piece in enumerate(across):
        pieces[2 * i + 2] = piece
        pieces[2 * i + 3] = swap(piece, "req", nreq, 1)

    own, sent, *weight = prefix(
        task_of, pieces, corpus_keys, vtc, task_keys, vtt, out_weight, kv, group
    )
    parts = list(merge(own, swap(sent, "req", nreq, 1), nreq // 2))
    for j in range(nreq // 2 - 1, 0, -1):
        parts[j] = swap(parts[j], "req", nreq, 2 * j)

    rows = queries.shape[0]
    columns = out_weight.shape[1] // nkvh
    attended = None
    came = []
    for bit in list(range(nkvh - 1, 0, -1)) + [0]:
        shape = jax.ShapeDtypeStruct((rows, columns), BF if bit else F32)
        if attended is None:
            attended, y = with_weight(
                functools.partial(combine_kernel, sources=len(parts), bit=bit),
                parts + list(hist),
                weight,
                [jax.ShapeDtypeStruct(queries.shape, BF), shape],
            )
        else:
            kernel = functools.partial(project_kernel, bit=bit)
            (y,) = with_weight(kernel, [attended], weight, [shape])
        came.append(swap(y, "kvh", nkvh, bit) if bit else y)
    total = came[-1]
    for y in came[:-1]:
        total = total + y.astype(F32)
    return total.astype(BF)


def solution(mesh):
    return jax.shard_map(
        shards,
        mesh=mesh,
        in_specs=(
            P("req", "kvh"),
            P("req", "kvh"),
            P("req", "kvh"),
            P("req", "kvh"),
            P("req", "kvh"),
            P("req", "kvh"),
            P("req", "kvh"),
            P("req"),
            P(),
            P("kvh", None),
        ),
        out_specs=P("req", "kvh"),
        check_vma=False,
    )
```

```python
import functools
import math

import jax
import jax.numpy as jnp
from jax import lax
from jax.experimental import pallas as pl
from jax.experimental.pallas import tpu as pltpu
from jax.sharding import PartitionSpec as P


HD = 128
HOLDERS = 2
LOG2 = math.log2(math.e) / math.sqrt(HD)
BIG = 1e30
COLS = 256
STEP = 1024
SUB = 512
CHUNKS = 8
AUG = 144
BF = jnp.bfloat16
F32 = jnp.float32


def dot_nt(a, b):
    return lax.dot_general(a, b, (((1,), (1,)), ((), ())), preferred_element_type=F32)


def dot_nn(a, b):
    return lax.dot_general(a, b, (((1,), (0,)), ((), ())), preferred_element_type=F32)


def split3(x):
    first = x.astype(BF)
    rest = x - first.astype(F32)
    second = rest.astype(BF)
    third = (rest - second.astype(F32)).astype(BF)
    return first, second, third


def iota(shape, axis):
    return lax.broadcasted_iota(jnp.int32, shape, axis)


def history_kernel(*refs, first, waves, hist, kv, group, turned):
    n_any = 4 + 2 * turned
    len_any, q_any, k_any, v_any, *value_any = refs[:n_any]
    o_ref, m_ref, l_ref, *targets = refs[n_any : n_any + 3 + 2 * turned]
    lengths, queries, q32, kbuf, vbuf, *rest = refs[n_any + 3 + 2 * turned :]
    value_bufs, sems = rest[:-1], rest[-1]
    heads = kv * group
    rows = o_ref.shape[0]
    per = rows // waves
    tall = per * hist
    small = [
        pltpu.make_async_copy(q_any.at[first : first + rows], queries, sems.at[0, waves + 1]),
        pltpu.make_async_copy(len_any, lengths, sems.at[1, waves + 1]),
    ]
    copies = []
    for w in range(waves):
        source = slice(first * hist + w * tall, first * hist + (w + 1) * tall)
        target = slice(w * tall, (w + 1) * tall)
        copies.append(
            [
                pltpu.make_async_copy(src.at[source], dst.at[target], sems.at[n, w])
                for n, (src, dst) in enumerate(((k_any, kbuf), (v_any, vbuf)))
            ]
        )
    turns = [
        pltpu.make_async_copy(src, dst, sems.at[n, waves])
        for n, (src, dst) in enumerate(zip(value_any, value_bufs))
    ]
    for group_of in [small] + copies + [turns]:
        for copy in group_of:
            copy.start()
    for copy in small:
        copy.wait()
    q32[...] = queries[...].astype(F32)
    row = iota((heads, HD), 0)
    for w in range(waves):
        for copy in copies[w]:
            copy.wait()
        ids = range(w * per, (w + 1) * per)
        scored = []
        for i in ids:
            wide = []
            for g in range(kv):
                q = jnp.zeros((heads, HD), F32)
                for h in range(g * group, (g + 1) * group):
                    line = q32[i : i + 1, h * HD : (h + 1) * HD]
                    q = jnp.where(row == h, jnp.broadcast_to(line, (heads, HD)), q)
                wide.append(q.astype(BF))
            s = dot_nt(jnp.concatenate(wide, 1), kbuf[i * hist : (i + 1) * hist, :])
            scored.append(jnp.where(iota(s.shape, 1) < lengths[first + i], s, -BIG))
        tops = [jnp.max(s, -1, keepdims=True) * LOG2 for s in scored]
        ps = [jnp.exp2(s * LOG2 - top) for s, top in zip(scored, tops)]
        totals = [jnp.sum(p, -1, keepdims=True) for p in ps]
        for i, p, top, total in zip(ids, ps, tops, totals):
            r = dot_nn(p.astype(BF), vbuf[i * hist : (i + 1) * hist, :])
            top = jnp.broadcast_to(top, (heads, HD))
            total = jnp.broadcast_to(total, (heads, HD))
            for h in range(heads):
                g = h // group
                to = slice(h * HD, (h + 1) * HD)
                o_ref[i : i + 1, to] = r[h : h + 1, g * HD : (g + 1) * HD]
                m_ref[i : i + 1, to] = top[h : h + 1]
                l_ref[i : i + 1, to] = total[h : h + 1]
    for copy, source, target in zip(turns, value_bufs, targets):
        copy.wait()
        for g in range(kv):
            for c in range(0, source.shape[0], STEP):
                target[g, :HD, c : c + STEP] = source[c : c + STEP, g * HD : (g + 1) * HD].T
            target[g, HD:, :] = jnp.ones((AUG - HD, source.shape[0]), BF)


def history(queries, keys, values, lengths, part, parts, turned, kv, group):
    rows, lanes = queries.shape[0] // parts, queries.shape[1]
    hist = keys.shape[0] // queries.shape[0]
    waves = rows // math.gcd(rows, 4)
    shape = jax.ShapeDtypeStruct((rows, lanes), F32)
    vmem = pl.BlockSpec(memory_space=pltpu.VMEM)
    operands = [lengths, queries, keys, values, *turned]
    return pl.pallas_call(
        functools.partial(
            history_kernel,
            first=part * rows,
            waves=waves,
            hist=hist,
            kv=kv,
            group=group,
            turned=len(turned) // 2,
        ),
        in_specs=[pl.BlockSpec(memory_space=pltpu.HBM)] * len(operands),
        out_specs=[vmem] * (3 + len(turned)),
        scratch_shapes=[
            pltpu.SMEM(lengths.shape, jnp.int32),
            pltpu.VMEM((rows, lanes), BF),
            pltpu.VMEM((rows, lanes), F32),
        ]
        + [pltpu.VMEM((rows * hist, kv * HD), BF)] * 2
        + [pltpu.VMEM(x.shape, BF) for x in turned]
        + [pltpu.SemaphoreType.DMA((2, waves + 2))],
        out_shape=[shape] * 3
        + [jax.ShapeDtypeStruct((kv, AUG, x.shape[0]), BF) for x in turned],
        compiler_params=pltpu.CompilerParams(vmem_limit_bytes=(12 if turned else 6) * 2**20),
        cost_estimate=pl.CostEstimate(
            flops=4 * rows * lanes * hist * kv,
            bytes_accessed=4 * rows * hist * kv * HD,
            transcendentals=0,
        ),
        name="history",
    )(*[pltpu.with_memory_space_constraint(x, pltpu.HBM) for x in operands])


def prefix_kernel(*refs, sources, rows, kv, group):
    task_row = refs[0]
    pieces = refs[1 : 1 + sources]
    ck, vtc, tk, vtt, weight = refs[1 + sources : 6 + sources]
    own_out, sent_out = refs[6 + sources : 8 + sources]
    kept = refs[8 + sources : 8 + sources + CHUNKS]
    q_all, qs, s_ref, acc_ref, m_ref, pay, sems = refs[8 + sources + CHUNKS :]
    tall = weight.shape[0] // CHUNKS
    fetches = [
        pltpu.make_async_copy(
            weight.at[i * tall : (i + 1) * tall], kept[i], sems.at[i]
        )
        for i in range(CHUNKS)
    ]
    for fetch in fetches:
        fetch.start()
    me = lax.axis_index("req")
    my_task = me // HOLDERS
    heads = kv * group
    lanes = heads * HD
    everyone = sources * rows
    part = COLS // group
    blocks = everyone // part

    square = (everyone, everyone)
    match = jnp.broadcast_to(task_row[...], (8, everyone)) == my_task
    count = dot_nn(match.astype(BF), (iota(square, 0) <= iota(square, 1)).astype(BF))
    live = jnp.sum(match.astype(F32), 1, keepdims=True)
    slot = jnp.where(match, count - 1.0, live + iota(count.shape, 1).astype(F32) - count)
    hot = (iota(square, 0) == slot[:1].astype(jnp.int32)).astype(F32)
    to_sorted = hot.astype(BF)
    from_sorted = hot.T.astype(BF)
    matched = jnp.sum((task_row[...] == my_task).astype(jnp.int32))
    task_blocks = (matched + part - 1) // part

    for j in range(sources):
        q_all[pl.ds(pl.multiple_of((me ^ j) * rows, rows), rows), :] = pieces[j][...]
    for g in range(kv):
        for h in range(group):
            at = (g * group + h) * HD
            if h % 2 == 0:
                both = dot_nn(to_sorted, q_all[:, at : at + 2 * HD]) * LOG2
            x = both[:, (h % 2) * HD : (h % 2 + 1) * HD]
            high = x.astype(BF)
            low = (x - high.astype(F32)).astype(BF)
            for b in range(blocks):
                qs[g * blocks + b, h * part : (h + 1) * part, :HD] = high[b * part : (b + 1) * part]
                qs[g * blocks + b, h * part : (h + 1) * part, HD:] = low[b * part : (b + 1) * part]

    def lane(g):
        return pl.ds(pl.multiple_of(g * HD, HD), HD)

    def scores(keys, start, g, index):
        k = keys[start : start + SUB, lane(g)]
        return dot_nt(jnp.concatenate([k, k], 1), qs[index])

    def fold(x, m8):
        x = jnp.max(x.reshape(-1, 8, COLS), 0)
        return x if m8 is None else jnp.maximum(m8, x)

    def stages(keys, vt, where_of, first_state, finish, count):
        n = keys.shape[0] // STEP

        def head(index, slot):
            b, g = where_of(index)
            m8 = None
            for c in range(0, STEP, SUB):
                s = scores(keys, c, g, b)
                s_ref[slot, c : c + SUB] = s
                m8 = fold(s, m8)
            return m8

        def body(i, m8):
            b, g = where_of(i)
            b_next, g_next = where_of(jnp.minimum(i + 1, count - 1))
            m, acc, valid = first_state(b)
            for stage in range(n):
                now, later = stage % 2, (stage + 1) % 2
                top = jnp.max(m8, 0, keepdims=True)
                new = top if m is None else jnp.maximum(m, top)
                if valid is not None:
                    new = jnp.where(valid, new, m)
                    shift = jnp.where(valid, new, BIG)
                else:
                    shift = new
                m8 = None
                r = None
                for c in range(0, STEP, SUB):
                    if stage + 1 < n:
                        s = scores(keys, (stage + 1) * STEP + c, g, b)
                    else:
                        s = scores(keys, c, g_next, b_next)
                    s_ref[later, c : c + SUB] = s
                    m8 = fold(s, m8)
                    p = jnp.exp2(s_ref[now, c : c + SUB] - shift).astype(BF)
                    at = stage * STEP + c
                    y = dot_nn(vt[g, :, at : at + SUB], p)
                    r = y if r is None else r + y
                acc = r if acc is None else acc * jnp.exp2(m - new) + r
                m = new
            finish(b, m, acc)
            return m8

        lax.fori_loop(0, count, body, head(0, 0))

    def keep(b, m, acc):
        acc_ref[b] = acc
        m_ref[b] = jnp.broadcast_to(m, (8, COLS))

    stages(ck, vtc, lambda i: (i, i // blocks), lambda b: (None, None, None), keep, kv * blocks)

    some = jnp.maximum(task_blocks, 1)

    def task_where(i):
        g = i // some
        return g * blocks + (i - g * some), g

    def task_state(b):
        request = lax.rem(b, blocks) * part + lax.rem(iota((1, COLS), 1), part)
        return m_ref[b][:1], acc_ref[b], request < matched

    @pl.when(task_blocks > 0)
    def _():
        stages(tk, vtt, task_where, task_state, keep, kv * task_blocks)

    pay[:, lanes:] = jnp.zeros((everyone, HD), BF)

    def emit(b, _):
        g = b // blocks
        at = pl.ds(pl.multiple_of(lax.rem(b, blocks) * part, part), part)
        acc = acc_ref[b]
        turned = acc[:HD].T.astype(BF)
        both = [x.astype(F32) for x in split3(m_ref[b][:1]) + split3(acc[HD : HD + 1])]
        stats = jnp.concatenate(both + [jnp.zeros((2, COLS), F32)], 0)
        stats = jnp.concatenate([stats] * (HD // 8), 0).T
        place = pay[at, lanes:].astype(F32)
        lane_head = iota((part, HD), 1) // 8
        for h in range(group):
            head = g * group + h
            pay[at, pl.ds(pl.multiple_of(head * HD, HD), HD)] = turned[h * part : (h + 1) * part]
            place = jnp.where(lane_head == head, stats[h * part : (h + 1) * part], place)
        pay[at, lanes:] = place.astype(BF)
        return 0

    lax.fori_loop(0, kv * blocks, emit, 0)
    for c in range(0, lanes + HD, 2 * HD):
        end = min(c + 2 * HD, lanes + HD)
        pay[:, c:end] = dot_nn(from_sorted, pay[:, c:end]).astype(BF)
    for j in range(sources):
        out = sent_out if j % 2 else own_out
        out[j // 2 * rows : (j // 2 + 1) * rows, :] = pay[
            pl.ds(pl.multiple_of((me ^ j) * rows, rows), rows), :
        ]
    for fetch in fetches:
        fetch.wait()


def prefix(task_of, pieces, ck, vtc, tk, vtt, weight, kv, group):
    sources = len(pieces)
    rows, lanes = pieces[0].shape
    everyone = sources * rows
    blocks = everyone * group // COLS
    vmem = pl.BlockSpec(memory_space=pltpu.VMEM)
    return pl.pallas_call(
        functools.partial(prefix_kernel, sources=sources, rows=rows, kv=kv, group=group),
        in_specs=[vmem] * (5 + sources) + [pl.BlockSpec(memory_space=pltpu.HBM)],
        out_specs=[vmem] * (2 + CHUNKS),
        out_shape=[jax.ShapeDtypeStruct((everyone // 2, lanes + HD), BF)] * 2
        + [pltpu.VMEM((weight.shape[0] // CHUNKS, weight.shape[1]), BF)] * CHUNKS,
        scratch_shapes=[
            pltpu.VMEM((everyone, lanes), BF),
            pltpu.VMEM((kv * blocks, COLS, 2 * HD), BF),
            pltpu.VMEM((2, STEP, COLS), F32),
            pltpu.VMEM((kv * blocks, AUG, COLS), F32),
            pltpu.VMEM((kv * blocks, 8, COLS), F32),
            pltpu.VMEM((everyone, lanes + HD), BF),
            pltpu.SemaphoreType.DMA((CHUNKS,)),
        ],
        compiler_params=pltpu.CompilerParams(vmem_limit_bytes=7 * 2**20),
        name="prefix",
    )(task_of[None, :], *pieces, ck, vtc, tk, vtt, weight)


def merge_kernel(a_ref, b_ref, *outs):
    rows, wide = a_ref.shape
    lanes = wide - HD
    part = rows // len(outs)
    row, col = iota((HD, HD), 0), iota((HD, HD), 1)
    same = row // 8 == col // 8
    take_m = (same & (row % 8 < 3)).astype(BF)
    take_l = (same & (row % 8 >= 3) & (row % 8 < 6)).astype(BF)
    spread = (iota((2 * HD, lanes), 0) % HD == iota((2 * HD, lanes), 1) // HD * 8).astype(BF)
    sa, sb = a_ref[:, lanes:], b_ref[:, lanes:]
    ma, mb = dot_nn(sa, take_m), dot_nn(sb, take_m)
    peak = jnp.maximum(ma, mb)
    fa, fb = jnp.exp2(ma - peak), jnp.exp2(mb - peak)
    total = dot_nn(sa, take_l) * fa + dot_nn(sb, take_l) * fb

    def widen(x):
        high = x.astype(BF)
        low = (x - high.astype(F32)).astype(BF)
        return dot_nn(jnp.concatenate([high, low], 1), spread)

    out = a_ref[:, :lanes].astype(F32) * widen(fa) + b_ref[:, :lanes].astype(F32) * widen(fb)
    out = out.astype(BF)
    place = iota(peak.shape, 1) % 8
    stats = jnp.zeros(peak.shape, F32)
    for i, x in enumerate(split3(peak) + split3(total)):
        stats = jnp.where(place == i, x.astype(F32), stats)
    stats = stats.astype(BF)
    for j, ref in enumerate(outs):
        ref[:, :lanes] = out[j * part : (j + 1) * part]
        ref[:, lanes:] = stats[j * part : (j + 1) * part]


def merge(a, b, pieces):
    shape = jax.ShapeDtypeStruct((a.shape[0] // pieces, a.shape[1]), BF)
    vmem = pl.BlockSpec(memory_space=pltpu.VMEM)
    return pl.pallas_call(
        merge_kernel,
        in_specs=[vmem] * 2,
        out_specs=[vmem] * pieces,
        out_shape=[shape] * pieces,
        compiler_params=pltpu.CompilerParams(vmem_limit_bytes=3 * 2**20),
        name="merge",
    )(a, b)


def product(bit, x, w_refs, o_ref):
    columns = o_ref.shape[1]
    at = pl.ds(pl.multiple_of((lax.axis_index("kvh") ^ bit) * columns, columns), columns)
    y = None
    for i, w_ref in enumerate(w_refs):
        tall = w_ref.shape[0]
        part = dot_nn(x[:, i * tall : (i + 1) * tall], w_ref[:, at])
        y = part if y is None else y + part
    o_ref[...] = y.astype(o_ref.dtype)


def combine_kernel(*refs, sources, bit):
    parts = refs[:sources]
    early, late = refs[sources : sources + 3], refs[sources + 3 : sources + 6]
    ho, hm, hl = [jnp.concatenate([a[...], b[...]], 0) for a, b in zip(early, late)]
    w_refs = refs[sources + 6 : -2]
    out, y_ref = refs[-2:]
    lanes = out.shape[1]
    row, col = iota((HD, lanes), 0), iota((HD, lanes), 1)
    same = row // 8 == col // HD
    take_m = (same & (row % 8 < 3)).astype(BF)
    take_l = (same & (row % 8 >= 3) & (row % 8 < 6)).astype(BF)
    tops = [dot_nn(x[:, lanes:], take_m) for x in parts]
    sums = [dot_nn(x[:, lanes:], take_l) for x in parts]
    peak = hm
    for top in tops:
        peak = jnp.maximum(peak, top)
    factor = jnp.exp2(hm - peak)
    num = ho * factor
    den = hl * factor
    for x, top, total in zip(parts, tops, sums):
        factor = jnp.exp2(top - peak)
        num = num + x[:, :lanes].astype(F32) * factor
        den = den + total * factor
    attended = (num / den).astype(BF)
    out[...] = attended
    product(bit, attended, w_refs, y_ref)


def project_kernel(x_ref, *refs, bit):
    product(bit, x_ref[...], refs[:-1], refs[-1])


def with_weight(kernel, operands, weight, shapes):
    vmem = pl.BlockSpec(memory_space=pltpu.VMEM)
    out = pl.pallas_call(
        kernel,
        in_specs=[vmem] * (len(operands) + len(weight)),
        out_specs=[vmem] * len(shapes),
        out_shape=shapes,
        compiler_params=pltpu.CompilerParams(vmem_limit_bytes=2 * 2**20),
    )(*operands, *weight)
    return out


def shards(
    queries,
    corpus_keys,
    corpus_values,
    task_keys,
    task_values,
    history_keys,
    history_values,
    history_lengths,
    task_of,
    out_weight,
):
    kv = corpus_keys.shape[1] // HD
    group = queries.shape[1] // HD // kv
    nreq, nkvh = lax.axis_size("req"), lax.axis_size("kvh")

    def swap(x, axis, size, bit):
        return lax.ppermute(x, axis, [(i, i ^ bit) for i in range(size)])

    pieces = [queries] + [None] * (nreq - 1)
    for bit in range(nreq - 2, 1, -2):
        pieces[bit] = swap(queries, "req", nreq, bit)

    def part_of_history(part, turned):
        return history(
            queries, history_keys, history_values, history_lengths, part, 2, turned, kv, group
        )

    *early, vtc, vtt = part_of_history(0, (corpus_values, task_values))
    passed, early, vtc, vtt = lax.optimization_barrier((pieces[::2], early, vtc, vtt))
    for i, piece in enumerate(passed):
        pieces[2 * i] = piece
        pieces[2 * i + 1] = swap(piece, "req", nreq, 1)

    own, sent, *weight = prefix(
        task_of, pieces, corpus_keys, vtc, task_keys, vtt, out_weight, kv, group
    )
    parts = list(merge(own, swap(sent, "req", nreq, 1), nreq // 2))
    late = part_of_history(1, ())
    for j in range(nreq // 2 - 1, 0, -1):
        parts[j] = swap(parts[j], "req", nreq, 2 * j)

    rows = queries.shape[0]
    columns = out_weight.shape[1] // nkvh
    attended = None
    came = []
    for bit in list(range(nkvh - 1, 0, -1)) + [0]:
        shape = jax.ShapeDtypeStruct((rows, columns), BF if bit else F32)
        if attended is None:
            attended, y = with_weight(
                functools.partial(combine_kernel, sources=len(parts), bit=bit),
                parts + list(early) + list(late),
                weight,
                [jax.ShapeDtypeStruct(queries.shape, BF), shape],
            )
        else:
            kernel = functools.partial(project_kernel, bit=bit)
            (y,) = with_weight(kernel, [attended], weight, [shape])
        came.append(swap(y, "kvh", nkvh, bit) if bit else y)
    total = came[-1]
    for y in came[:-1]:
        total = total + y.astype(F32)
    return total.astype(BF)


def solution(mesh):
    return jax.shard_map(
        shards,
        mesh=mesh,
        in_specs=(
            P("req", "kvh"),
            P("req", "kvh"),
            P("req", "kvh"),
            P("req", "kvh"),
            P("req", "kvh"),
            P("req", "kvh"),
            P("req", "kvh"),
            P("req"),
            P(),
            P("kvh", None),
        ),
        out_specs=P("req", "kvh"),
        check_vma=False,
    )
```

```python
import functools
import math

import jax
import jax.numpy as jnp
from jax import lax
from jax.experimental import pallas as pl
from jax.experimental.pallas import tpu as pltpu
from jax.sharding import PartitionSpec as P


HD = 128
HOLDERS = 2
LOG2 = math.log2(math.e) / math.sqrt(HD)
BIG = 1e30
COLS = 256
STEP = 1024
SUB = 512
CHUNKS = 8
UNROLL = 4
EMIT = 4
AUG = 144
BF = jnp.bfloat16
F32 = jnp.float32


def dot_nt(a, b):
    return lax.dot_general(a, b, (((1,), (1,)), ((), ())), preferred_element_type=F32)


def dot_nn(a, b):
    return lax.dot_general(a, b, (((1,), (0,)), ((), ())), preferred_element_type=F32)


GATHER = (6, 4, 2)
SEND = (3, 2, 1)


def order(size, first):
    first = [bit for bit in first if bit < size]
    return first + [bit for bit in range(1, size) if bit not in first]


def chip_order(size, first):
    return [2 * bit for bit in order(size // 2, [bit // 2 for bit in first])]


def split3(x):
    first = x.astype(BF)
    rest = x - first.astype(F32)
    second = rest.astype(BF)
    third = (rest - second.astype(F32)).astype(BF)
    return first, second, third


def iota(shape, axis):
    return lax.broadcasted_iota(jnp.int32, shape, axis)


def history_kernel(
    len_any, q_any, k_any, v_any, o_ref, m_ref, l_ref, lengths, queries, q32, kbuf, vbuf, sems,
    *, first, waves, hist, kv, group
):
    heads = kv * group
    rows = o_ref.shape[0]
    per = rows // waves
    tall = per * hist
    small = [
        pltpu.make_async_copy(q_any.at[first : first + rows], queries, sems.at[0, waves]),
        pltpu.make_async_copy(len_any, lengths, sems.at[1, waves]),
    ]
    copies = []
    for w in range(waves):
        source = slice(first * hist + w * tall, first * hist + (w + 1) * tall)
        target = slice(w * tall, (w + 1) * tall)
        copies.append(
            [
                pltpu.make_async_copy(src.at[source], dst.at[target], sems.at[n, w])
                for n, (src, dst) in enumerate(((k_any, kbuf), (v_any, vbuf)))
            ]
        )
    for group_of in [small] + copies:
        for copy in group_of:
            copy.start()
    for copy in small:
        copy.wait()
    q32[...] = queries[...].astype(F32)
    row = iota((heads, HD), 0)
    for w in range(waves):
        for copy in copies[w]:
            copy.wait()
        ids = range(w * per, (w + 1) * per)
        scored = []
        for i in ids:
            wide = []
            for g in range(kv):
                q = jnp.zeros((heads, HD), F32)
                for h in range(g * group, (g + 1) * group):
                    line = q32[i : i + 1, h * HD : (h + 1) * HD]
                    q = jnp.where(row == h, jnp.broadcast_to(line, (heads, HD)), q)
                wide.append(q.astype(BF))
            s = dot_nt(jnp.concatenate(wide, 1), kbuf[i * hist : (i + 1) * hist, :])
            scored.append(jnp.where(iota(s.shape, 1) < lengths[first + i], s, -BIG))
        tops = [jnp.max(s, -1, keepdims=True) * LOG2 for s in scored]
        ps = [jnp.exp2(s * LOG2 - top) for s, top in zip(scored, tops)]
        totals = [jnp.sum(p, -1, keepdims=True) for p in ps]
        for i, p, top, total in zip(ids, ps, tops, totals):
            r = dot_nn(p.astype(BF), vbuf[i * hist : (i + 1) * hist, :])
            top = jnp.broadcast_to(top, (heads, HD))
            total = jnp.broadcast_to(total, (heads, HD))
            for h in range(heads):
                g = h // group
                to = slice(h * HD, (h + 1) * HD)
                o_ref[i : i + 1, to] = r[h : h + 1, g * HD : (g + 1) * HD]
                m_ref[i : i + 1, to] = top[h : h + 1]
                l_ref[i : i + 1, to] = total[h : h + 1]


def turn_kernel(cv, tv, vtc, vtt, *, kv):
    for source, target in ((cv, vtc), (tv, vtt)):
        for g in range(kv):
            for c in range(0, source.shape[0], STEP):
                target[g, :HD, c : c + STEP] = source[c : c + STEP, g * HD : (g + 1) * HD].T
            target[g, HD:, :] = jnp.ones((AUG - HD, source.shape[0]), BF)


def turn(values, kv):
    vmem = pl.BlockSpec(memory_space=pltpu.VMEM)
    return pl.pallas_call(
        functools.partial(turn_kernel, kv=kv),
        in_specs=[vmem] * len(values),
        out_specs=[vmem] * len(values),
        out_shape=[jax.ShapeDtypeStruct((kv, AUG, x.shape[0]), BF) for x in values],
        compiler_params=pltpu.CompilerParams(vmem_limit_bytes=4 * 2**20),
        name="turn",
    )(*values)


def history(queries, keys, values, lengths, part, parts, kv, group):
    rows, lanes = queries.shape[0] // parts, queries.shape[1]
    hist = keys.shape[0] // queries.shape[0]
    waves = rows // math.gcd(rows, 4)
    shape = jax.ShapeDtypeStruct((rows, lanes), F32)
    vmem = pl.BlockSpec(memory_space=pltpu.VMEM)
    operands = [lengths, queries, keys, values]
    return pl.pallas_call(
        functools.partial(
            history_kernel,
            first=part * rows,
            waves=waves,
            hist=hist,
            kv=kv,
            group=group,
        ),
        in_specs=[pl.BlockSpec(memory_space=pltpu.HBM)] * len(operands),
        out_specs=[vmem] * 3,
        scratch_shapes=[
            pltpu.SMEM(lengths.shape, jnp.int32),
            pltpu.VMEM((rows, lanes), BF),
            pltpu.VMEM((rows, lanes), F32),
        ]
        + [pltpu.VMEM((rows * hist, kv * HD), BF)] * 2
        + [pltpu.SemaphoreType.DMA((2, waves + 1))],
        out_shape=[shape] * 3,
        compiler_params=pltpu.CompilerParams(vmem_limit_bytes=6 * 2**20),
        cost_estimate=pl.CostEstimate(
            flops=4 * rows * lanes * hist * kv,
            bytes_accessed=4 * rows * hist * kv * HD,
            transcendentals=0,
        ),
        name="history",
    )(*[pltpu.with_memory_space_constraint(x, pltpu.HBM) for x in operands])


def prefix_kernel(*refs, sources, rows, kv, group):
    task_row = refs[0]
    pieces = refs[1 : 1 + sources]
    ck, vtc, tk, vtt, weight = refs[1 + sources : 6 + sources]
    own_out, sent_out = refs[6 + sources : 8 + sources]
    kept = refs[8 + sources : 8 + sources + CHUNKS]
    q_all, qs, s_ref, acc_ref, m_ref, pay, sems = refs[8 + sources + CHUNKS :]
    tall = weight.shape[0] // CHUNKS
    fetches = [
        pltpu.make_async_copy(
            weight.at[i * tall : (i + 1) * tall], kept[i], sems.at[i]
        )
        for i in range(CHUNKS)
    ]
    for fetch in fetches:
        fetch.start()
    me = lax.axis_index("req")
    my_task = me // HOLDERS
    heads = kv * group
    lanes = heads * HD
    everyone = sources * rows
    part = COLS // group
    blocks = everyone // part

    square = (everyone, everyone)
    match = jnp.broadcast_to(task_row[...], (8, everyone)) == my_task
    count = dot_nn(match.astype(BF), (iota(square, 0) <= iota(square, 1)).astype(BF))
    live = jnp.sum(match.astype(F32), 1, keepdims=True)
    slot = jnp.where(match, count - 1.0, live + iota(count.shape, 1).astype(F32) - count)
    hot = (iota(square, 0) == slot[:1].astype(jnp.int32)).astype(F32)
    to_sorted = hot.astype(BF)
    from_sorted = hot.T.astype(BF)
    matched = jnp.sum((task_row[...] == my_task).astype(jnp.int32))
    task_blocks = (matched + part - 1) // part

    for j in range(sources):
        q_all[pl.ds(pl.multiple_of((me ^ j) * rows, rows), rows), :] = pieces[j][...]
    for g in range(kv):
        for h in range(group):
            at = (g * group + h) * HD
            if h % 2 == 0:
                both = dot_nn(to_sorted, q_all[:, at : at + 2 * HD]) * LOG2
            x = both[:, (h % 2) * HD : (h % 2 + 1) * HD]
            high = x.astype(BF)
            low = (x - high.astype(F32)).astype(BF)
            for b in range(blocks):
                qs[g * blocks + b, h * part : (h + 1) * part, :HD] = high[b * part : (b + 1) * part]
                qs[g * blocks + b, h * part : (h + 1) * part, HD:] = low[b * part : (b + 1) * part]

    def lane(g):
        return pl.ds(pl.multiple_of(g * HD, HD), HD)

    def scores(keys, start, g, index):
        k = keys[start : start + SUB, lane(g)]
        return dot_nt(jnp.concatenate([k, k], 1), qs[index])

    def fold(x, m8):
        x = jnp.max(x.reshape(-1, 8, COLS), 0)
        return x if m8 is None else jnp.maximum(m8, x)

    def stages(keys, vt, where_of, first_state, finish, turns, inner):
        n = keys.shape[0] // STEP

        def head(slot):
            b, g = where_of(0, 0)
            m8 = None
            for c in range(0, STEP, SUB):
                s = scores(keys, c, g, b)
                s_ref[slot, c : c + SUB] = s
                m8 = fold(s, m8)
            return m8

        def one(i, u, m8):
            b, g = where_of(i, u)
            last = u + 1 == inner
            b_next, g_next = where_of(jnp.minimum(i + 1, turns - 1) if last else i, 0 if last else u + 1)
            m, acc, valid = first_state(b)
            for stage in range(n):
                now, later = stage % 2, (stage + 1) % 2
                top = jnp.max(m8, 0, keepdims=True)
                new = top if m is None else jnp.maximum(m, top)
                if valid is not None:
                    new = jnp.where(valid, new, m)
                    shift = jnp.where(valid, new, BIG)
                else:
                    shift = new
                m8 = None
                r = None
                for c in range(0, STEP, SUB):
                    if stage + 1 < n:
                        s = scores(keys, (stage + 1) * STEP + c, g, b)
                    else:
                        s = scores(keys, c, g_next, b_next)
                    s_ref[later, c : c + SUB] = s
                    m8 = fold(s, m8)
                    p = jnp.exp2(s_ref[now, c : c + SUB] - shift).astype(BF)
                    at = stage * STEP + c
                    y = dot_nn(vt[g, :, at : at + SUB], p)
                    r = y if r is None else r + y
                acc = r if acc is None else acc * jnp.exp2(m - new) + r
                m = new
            finish(b, m, acc)
            return m8

        def body(i, m8):
            for u in range(inner):
                m8 = one(i, u, m8)
            return m8

        lax.fori_loop(0, turns, body, head(0))

    def keep(b, m, acc):
        acc_ref[b] = acc
        m_ref[b] = jnp.broadcast_to(m, (8, COLS))

    def corpus_where(i, u):
        item = i * inner + u
        return item, item // blocks

    inner = math.gcd(UNROLL, kv * blocks)
    stages(ck, vtc, corpus_where, lambda b: (None, None, None), keep, kv * blocks // inner, inner)

    def task_where(i, u):
        return u * blocks + i, u

    def task_state(b):
        request = lax.rem(b, blocks) * part + lax.rem(iota((1, COLS), 1), part)
        return m_ref[b][:1], acc_ref[b], request < matched

    @pl.when(task_blocks > 0)
    def _():
        stages(tk, vtt, task_where, task_state, keep, task_blocks, kv)

    pay[:, lanes:] = jnp.zeros((everyone, HD), BF)

    def emit(b, _):
        g = b // blocks
        at = pl.ds(pl.multiple_of(lax.rem(b, blocks) * part, part), part)
        acc = acc_ref[b]
        turned = acc[:HD].T.astype(BF)
        both = [x.astype(F32) for x in split3(m_ref[b][:1]) + split3(acc[HD : HD + 1])]
        stats = jnp.concatenate(both + [jnp.zeros((2, COLS), F32)], 0)
        stats = jnp.concatenate([stats] * (HD // 8), 0).T
        place = pay[at, lanes:].astype(F32)
        lane_head = iota((part, HD), 1) // 8
        for h in range(group):
            head = g * group + h
            pay[at, pl.ds(pl.multiple_of(head * HD, HD), HD)] = turned[h * part : (h + 1) * part]
            place = jnp.where(lane_head == head, stats[h * part : (h + 1) * part], place)
        pay[at, lanes:] = place.astype(BF)
        return 0

    lax.fori_loop(0, kv * blocks, emit, 0, unroll=EMIT)
    for c in range(0, lanes + HD, 2 * HD):
        end = min(c + 2 * HD, lanes + HD)
        pay[:, c:end] = dot_nn(from_sorted, pay[:, c:end]).astype(BF)
    for j in range(sources):
        out = sent_out if j % 2 else own_out
        out[j // 2 * rows : (j // 2 + 1) * rows, :] = pay[
            pl.ds(pl.multiple_of((me ^ j) * rows, rows), rows), :
        ]
    for fetch in fetches:
        fetch.wait()


def prefix(task_of, pieces, ck, vtc, tk, vtt, weight, kv, group):
    sources = len(pieces)
    rows, lanes = pieces[0].shape
    everyone = sources * rows
    blocks = everyone * group // COLS
    vmem = pl.BlockSpec(memory_space=pltpu.VMEM)
    return pl.pallas_call(
        functools.partial(prefix_kernel, sources=sources, rows=rows, kv=kv, group=group),
        in_specs=[vmem] * (5 + sources) + [pl.BlockSpec(memory_space=pltpu.HBM)],
        out_specs=[vmem] * (2 + CHUNKS),
        out_shape=[jax.ShapeDtypeStruct((everyone // 2, lanes + HD), BF)] * 2
        + [pltpu.VMEM((weight.shape[0] // CHUNKS, weight.shape[1]), BF)] * CHUNKS,
        scratch_shapes=[
            pltpu.VMEM((everyone, lanes), BF),
            pltpu.VMEM((kv * blocks, COLS, 2 * HD), BF),
            pltpu.VMEM((2, STEP, COLS), F32),
            pltpu.VMEM((kv * blocks, AUG, COLS), F32),
            pltpu.VMEM((kv * blocks, 8, COLS), F32),
            pltpu.VMEM((everyone, lanes + HD), BF),
            pltpu.SemaphoreType.DMA((CHUNKS,)),
        ],
        compiler_params=pltpu.CompilerParams(vmem_limit_bytes=7 * 2**20),
        name="prefix",
    )(task_of[None, :], *pieces, ck, vtc, tk, vtt, weight)


def merge_kernel(a_ref, b_ref, *outs):
    rows, wide = a_ref.shape
    lanes = wide - HD
    part = rows // len(outs)
    row, col = iota((HD, HD), 0), iota((HD, HD), 1)
    same = row // 8 == col // 8
    take_m = (same & (row % 8 < 3)).astype(BF)
    take_l = (same & (row % 8 >= 3) & (row % 8 < 6)).astype(BF)
    spread = (iota((2 * HD, lanes), 0) % HD == iota((2 * HD, lanes), 1) // HD * 8).astype(BF)
    sa, sb = a_ref[:, lanes:], b_ref[:, lanes:]
    ma, mb = dot_nn(sa, take_m), dot_nn(sb, take_m)
    peak = jnp.maximum(ma, mb)
    fa, fb = jnp.exp2(ma - peak), jnp.exp2(mb - peak)
    total = dot_nn(sa, take_l) * fa + dot_nn(sb, take_l) * fb

    def widen(x):
        high = x.astype(BF)
        low = (x - high.astype(F32)).astype(BF)
        return dot_nn(jnp.concatenate([high, low], 1), spread)

    out = a_ref[:, :lanes].astype(F32) * widen(fa) + b_ref[:, :lanes].astype(F32) * widen(fb)
    out = out.astype(BF)
    place = iota(peak.shape, 1) % 8
    stats = jnp.zeros(peak.shape, F32)
    for i, x in enumerate(split3(peak) + split3(total)):
        stats = jnp.where(place == i, x.astype(F32), stats)
    stats = stats.astype(BF)
    for j, ref in enumerate(outs):
        ref[:, :lanes] = out[j * part : (j + 1) * part]
        ref[:, lanes:] = stats[j * part : (j + 1) * part]


def merge(a, b, pieces):
    shape = jax.ShapeDtypeStruct((a.shape[0] // pieces, a.shape[1]), BF)
    vmem = pl.BlockSpec(memory_space=pltpu.VMEM)
    return pl.pallas_call(
        merge_kernel,
        in_specs=[vmem] * 2,
        out_specs=[vmem] * pieces,
        out_shape=[shape] * pieces,
        compiler_params=pltpu.CompilerParams(vmem_limit_bytes=3 * 2**20),
        name="merge",
    )(a, b)


def product(bit, x, w_refs, o_ref):
    columns = o_ref.shape[1]
    at = pl.ds(pl.multiple_of((lax.axis_index("kvh") ^ bit) * columns, columns), columns)
    y = None
    for i, w_ref in enumerate(w_refs):
        tall = w_ref.shape[0]
        part = dot_nn(x[:, i * tall : (i + 1) * tall], w_ref[:, at])
        y = part if y is None else y + part
    o_ref[...] = y.astype(o_ref.dtype)


def combine_kernel(*refs, sources, bit):
    parts = refs[:sources]
    early, late = refs[sources : sources + 3], refs[sources + 3 : sources + 6]
    ho, hm, hl = [jnp.concatenate([a[...], b[...]], 0) for a, b in zip(early, late)]
    w_refs = refs[sources + 6 : -2]
    out, y_ref = refs[-2:]
    lanes = out.shape[1]
    row, col = iota((HD, lanes), 0), iota((HD, lanes), 1)
    same = row // 8 == col // HD
    take_m = (same & (row % 8 < 3)).astype(BF)
    take_l = (same & (row % 8 >= 3) & (row % 8 < 6)).astype(BF)
    tops = [dot_nn(x[:, lanes:], take_m) for x in parts]
    sums = [dot_nn(x[:, lanes:], take_l) for x in parts]
    peak = hm
    for top in tops:
        peak = jnp.maximum(peak, top)
    factor = jnp.exp2(hm - peak)
    num = ho * factor
    den = hl * factor
    for x, top, total in zip(parts, tops, sums):
        factor = jnp.exp2(top - peak)
        num = num + x[:, :lanes].astype(F32) * factor
        den = den + total * factor
    attended = (num / den).astype(BF)
    out[...] = attended
    product(bit, attended, w_refs, y_ref)


def project_kernel(x_ref, *refs, bit):
    product(bit, x_ref[...], refs[:-1], refs[-1])


def with_weight(kernel, operands, weight, shapes):
    vmem = pl.BlockSpec(memory_space=pltpu.VMEM)
    out = pl.pallas_call(
        kernel,
        in_specs=[vmem] * (len(operands) + len(weight)),
        out_specs=[vmem] * len(shapes),
        out_shape=shapes,
        compiler_params=pltpu.CompilerParams(vmem_limit_bytes=2 * 2**20),
    )(*operands, *weight)
    return out


def shards(
    queries,
    corpus_keys,
    corpus_values,
    task_keys,
    task_values,
    history_keys,
    history_values,
    history_lengths,
    task_of,
    out_weight,
):
    kv = corpus_keys.shape[1] // HD
    group = queries.shape[1] // HD // kv
    nreq, nkvh = lax.axis_size("req"), lax.axis_size("kvh")

    def swap(x, axis, size, bit):
        return lax.ppermute(x, axis, [(i, i ^ bit) for i in range(size)])

    pieces = [queries] + [None] * (nreq - 1)
    for bit in chip_order(nreq, GATHER):
        pieces[bit] = swap(queries, "req", nreq, bit)

    def part_of_history(part):
        return history(queries, history_keys, history_values, history_lengths, part, 2, kv, group)

    early = part_of_history(0)
    passed, early = lax.optimization_barrier((pieces[::2], early))
    for i, piece in enumerate(passed):
        pieces[2 * i] = piece
        pieces[2 * i + 1] = swap(piece, "req", nreq, 1)
    vtc, vtt = turn((corpus_values, task_values), kv)

    own, sent, *weight = prefix(
        task_of, pieces, corpus_keys, vtc, task_keys, vtt, out_weight, kv, group
    )
    parts = list(merge(own, swap(sent, "req", nreq, 1), nreq // 2))
    late = part_of_history(1)
    for j in range(nreq // 2 - 1, 0, -1):
        parts[j] = swap(parts[j], "req", nreq, 2 * j)

    rows = queries.shape[0]
    columns = out_weight.shape[1] // nkvh
    attended = None
    came = []
    for bit in order(nkvh, SEND) + [0]:
        shape = jax.ShapeDtypeStruct((rows, columns), BF if bit else F32)
        if attended is None:
            attended, y = with_weight(
                functools.partial(combine_kernel, sources=len(parts), bit=bit),
                parts + list(early) + list(late),
                weight,
                [jax.ShapeDtypeStruct(queries.shape, BF), shape],
            )
        else:
            kernel = functools.partial(project_kernel, bit=bit)
            (y,) = with_weight(kernel, [attended], weight, [shape])
        came.append(swap(y, "kvh", nkvh, bit) if bit else y)
    total = came[-1]
    for y in came[:-1]:
        total = total + y.astype(F32)
    return total.astype(BF)


def solution(mesh):
    return jax.shard_map(
        shards,
        mesh=mesh,
        in_specs=(
            P("req", "kvh"),
            P("req", "kvh"),
            P("req", "kvh"),
            P("req", "kvh"),
            P("req", "kvh"),
            P("req", "kvh"),
            P("req", "kvh"),
            P("req"),
            P(),
            P("kvh", None),
        ),
        out_specs=P("req", "kvh"),
        check_vma=False,
    )
```

```python
import functools
import math

import jax
import jax.numpy as jnp
from jax import lax
from jax.experimental import pallas as pl
from jax.experimental.pallas import tpu as pltpu
from jax.sharding import PartitionSpec as P


HD = 128
HOLDERS = 2
LOG2 = math.log2(math.e) / math.sqrt(HD)
BIG = 1e30
COLS = 256
STEP = 1024
SUB = 512
CHUNKS = 8
UNROLL = 4
EMIT = 4
AUG = 144
BF = jnp.bfloat16
F32 = jnp.float32


def dot_nt(a, b):
    return lax.dot_general(a, b, (((1,), (1,)), ((), ())), preferred_element_type=F32)


def dot_nn(a, b):
    return lax.dot_general(a, b, (((1,), (0,)), ((), ())), preferred_element_type=F32)


GATHER = (6, 4, 2)
SEND = (3, 2, 1)


def order(size, first):
    first = [bit for bit in first if bit < size]
    return first + [bit for bit in range(1, size) if bit not in first]


def chip_order(size, first):
    return [2 * bit for bit in order(size // 2, [bit // 2 for bit in first])]


def split3(x):
    first = x.astype(BF)
    rest = x - first.astype(F32)
    second = rest.astype(BF)
    third = (rest - second.astype(F32)).astype(BF)
    return first, second, third


def iota(shape, axis):
    return lax.broadcasted_iota(jnp.int32, shape, axis)


def history_kernel(
    len_any, q_any, k_any, v_any, o_ref, m_ref, l_ref, lengths, queries, q32, kbuf, vbuf, sems,
    *, first, waves, hist, kv, group
):
    heads = kv * group
    rows = o_ref.shape[0]
    per = rows // waves
    tall = per * hist
    small = [
        pltpu.make_async_copy(q_any.at[first : first + rows], queries, sems.at[0, waves]),
        pltpu.make_async_copy(len_any, lengths, sems.at[1, waves]),
    ]
    copies = []
    for w in range(waves):
        source = slice(first * hist + w * tall, first * hist + (w + 1) * tall)
        target = slice(w * tall, (w + 1) * tall)
        copies.append(
            [
                pltpu.make_async_copy(src.at[source], dst.at[target], sems.at[n, w])
                for n, (src, dst) in enumerate(((k_any, kbuf), (v_any, vbuf)))
            ]
        )
    for group_of in [small] + copies:
        for copy in group_of:
            copy.start()
    for copy in small:
        copy.wait()
    q32[...] = queries[...].astype(F32)
    row = iota((heads, HD), 0)
    for w in range(waves):
        for copy in copies[w]:
            copy.wait()
        ids = range(w * per, (w + 1) * per)
        scored = []
        for i in ids:
            wide = []
            for g in range(kv):
                q = jnp.zeros((heads, HD), F32)
                for h in range(g * group, (g + 1) * group):
                    line = q32[i : i + 1, h * HD : (h + 1) * HD]
                    q = jnp.where(row == h, jnp.broadcast_to(line, (heads, HD)), q)
                wide.append(q.astype(BF))
            s = dot_nt(jnp.concatenate(wide, 1), kbuf[i * hist : (i + 1) * hist, :])
            scored.append(jnp.where(iota(s.shape, 1) < lengths[first + i], s, -BIG))
        tops = [jnp.max(s, -1, keepdims=True) * LOG2 for s in scored]
        ps = [jnp.exp2(s * LOG2 - top) for s, top in zip(scored, tops)]
        totals = [jnp.sum(p, -1, keepdims=True) for p in ps]
        for i, p, top, total in zip(ids, ps, tops, totals):
            r = dot_nn(p.astype(BF), vbuf[i * hist : (i + 1) * hist, :])
            top = jnp.broadcast_to(top, (heads, HD))
            total = jnp.broadcast_to(total, (heads, HD))
            for h in range(heads):
                g = h // group
                to = slice(h * HD, (h + 1) * HD)
                o_ref[i : i + 1, to] = r[h : h + 1, g * HD : (g + 1) * HD]
                m_ref[i : i + 1, to] = top[h : h + 1]
                l_ref[i : i + 1, to] = total[h : h + 1]


def turn_kernel(cv, tv, vtc, vtt, *, kv):
    for source, target in ((cv, vtc), (tv, vtt)):
        for g in range(kv):
            for c in range(0, source.shape[0], STEP):
                target[g, :HD, c : c + STEP] = source[c : c + STEP, g * HD : (g + 1) * HD].T
            target[g, HD:, :] = jnp.ones((AUG - HD, source.shape[0]), BF)


def turn(values, kv):
    vmem = pl.BlockSpec(memory_space=pltpu.VMEM)
    return pl.pallas_call(
        functools.partial(turn_kernel, kv=kv),
        in_specs=[vmem] * len(values),
        out_specs=[vmem] * len(values),
        out_shape=[jax.ShapeDtypeStruct((kv, AUG, x.shape[0]), BF) for x in values],
        compiler_params=pltpu.CompilerParams(vmem_limit_bytes=4 * 2**20),
        name="turn",
    )(*values)


def history(queries, keys, values, lengths, part, parts, kv, group):
    rows, lanes = queries.shape[0] // parts, queries.shape[1]
    hist = keys.shape[0] // queries.shape[0]
    waves = rows // math.gcd(rows, 4)
    shape = jax.ShapeDtypeStruct((rows, lanes), F32)
    vmem = pl.BlockSpec(memory_space=pltpu.VMEM)
    operands = [lengths, queries, keys, values]
    return pl.pallas_call(
        functools.partial(
            history_kernel,
            first=part * rows,
            waves=waves,
            hist=hist,
            kv=kv,
            group=group,
        ),
        in_specs=[pl.BlockSpec(memory_space=pltpu.HBM)] * len(operands),
        out_specs=[vmem] * 3,
        scratch_shapes=[
            pltpu.SMEM(lengths.shape, jnp.int32),
            pltpu.VMEM((rows, lanes), BF),
            pltpu.VMEM((rows, lanes), F32),
        ]
        + [pltpu.VMEM((rows * hist, kv * HD), BF)] * 2
        + [pltpu.SemaphoreType.DMA((2, waves + 1))],
        out_shape=[shape] * 3,
        compiler_params=pltpu.CompilerParams(vmem_limit_bytes=6 * 2**20),
        cost_estimate=pl.CostEstimate(
            flops=4 * rows * lanes * hist * kv,
            bytes_accessed=4 * rows * hist * kv * HD,
            transcendentals=0,
        ),
        name="history",
    )(*[pltpu.with_memory_space_constraint(x, pltpu.HBM) for x in operands])


def prefix_kernel(*refs, sources, rows, kv, group):
    task_row = refs[0]
    pieces = refs[1 : 1 + sources]
    ck, vtc, tk, vtt, weight = refs[1 + sources : 6 + sources]
    own_out, sent_out = refs[6 + sources : 8 + sources]
    kept = refs[8 + sources : 8 + sources + CHUNKS]
    q_all, qs, s_ref, acc_ref, m_ref, pay, back, sems = refs[8 + sources + CHUNKS :]
    tall = weight.shape[0] // CHUNKS
    fetches = [
        pltpu.make_async_copy(
            weight.at[i * tall : (i + 1) * tall], kept[i], sems.at[i]
        )
        for i in range(CHUNKS)
    ]
    for fetch in fetches:
        fetch.start()
    me = lax.axis_index("req")
    my_task = me // HOLDERS
    heads = kv * group
    lanes = heads * HD
    everyone = sources * rows
    part = COLS // group
    blocks = everyone // part

    square = (everyone, everyone)
    match = jnp.broadcast_to(task_row[...], (8, everyone)) == my_task
    count = dot_nn(match.astype(BF), (iota(square, 0) <= iota(square, 1)).astype(BF))
    live = jnp.sum(match.astype(F32), 1, keepdims=True)
    slot = jnp.where(match, count - 1.0, live + iota(count.shape, 1).astype(F32) - count)
    hot = (iota(square, 0) == slot[:1].astype(jnp.int32)).astype(F32)
    to_sorted = hot.astype(BF)
    back[...] = hot.T.astype(BF)
    matched = jnp.sum((task_row[...] == my_task).astype(jnp.int32))
    task_blocks = (matched + part - 1) // part

    for j in range(sources):
        q_all[pl.ds(pl.multiple_of((me ^ j) * rows, rows), rows), :] = pieces[j][...]
    for g in range(kv):
        for h in range(group):
            at = (g * group + h) * HD
            if h % 2 == 0:
                both = dot_nn(to_sorted, q_all[:, at : at + 2 * HD]) * LOG2
            x = both[:, (h % 2) * HD : (h % 2 + 1) * HD]
            high = x.astype(BF)
            low = (x - high.astype(F32)).astype(BF)
            for b in range(blocks):
                qs[g * blocks + b, h * part : (h + 1) * part, :HD] = high[b * part : (b + 1) * part]
                qs[g * blocks + b, h * part : (h + 1) * part, HD:] = low[b * part : (b + 1) * part]

    def lane(g):
        return pl.ds(pl.multiple_of(g * HD, HD), HD)

    def scores(keys, start, g, index):
        k = keys[start : start + SUB, lane(g)]
        return dot_nt(jnp.concatenate([k, k], 1), qs[index])

    def fold(x, m8):
        x = jnp.max(x.reshape(-1, 8, COLS), 0)
        return x if m8 is None else jnp.maximum(m8, x)

    def stages(keys, vt, where_of, first_state, finish, turns, inner):
        n = keys.shape[0] // STEP

        def head(slot):
            b, g = where_of(0, 0)
            m8 = None
            for c in range(0, STEP, SUB):
                s = scores(keys, c, g, b)
                s_ref[slot, c : c + SUB] = s
                m8 = fold(s, m8)
            return m8

        def one(i, u, m8):
            b, g = where_of(i, u)
            last = u + 1 == inner
            b_next, g_next = where_of(jnp.minimum(i + 1, turns - 1) if last else i, 0 if last else u + 1)
            m, acc, valid = first_state(b)
            for stage in range(n):
                now, later = stage % 2, (stage + 1) % 2
                top = jnp.max(m8, 0, keepdims=True)
                new = top if m is None else jnp.maximum(m, top)
                if valid is not None:
                    new = jnp.where(valid, new, m)
                    shift = jnp.where(valid, new, BIG)
                else:
                    shift = new
                m8 = None
                r = None
                for c in range(0, STEP, SUB):
                    if stage + 1 < n:
                        s = scores(keys, (stage + 1) * STEP + c, g, b)
                    else:
                        s = scores(keys, c, g_next, b_next)
                    s_ref[later, c : c + SUB] = s
                    m8 = fold(s, m8)
                    p = jnp.exp2(s_ref[now, c : c + SUB] - shift).astype(BF)
                    at = stage * STEP + c
                    y = dot_nn(vt[g, :, at : at + SUB], p)
                    r = y if r is None else r + y
                acc = r if acc is None else acc * jnp.exp2(m - new) + r
                m = new
            finish(b, m, acc)
            return m8

        def body(i, m8):
            for u in range(inner):
                m8 = one(i, u, m8)
            return m8

        lax.fori_loop(0, turns, body, head(0))

    def keep(b, m, acc):
        acc_ref[b] = acc
        m_ref[b] = jnp.broadcast_to(m, (8, COLS))

    def corpus_where(i, u):
        item = i * inner + u
        return item, item // blocks

    inner = math.gcd(UNROLL, kv * blocks)
    stages(ck, vtc, corpus_where, lambda b: (None, None, None), keep, kv * blocks // inner, inner)

    def task_where(i, u):
        return u * blocks + i, u

    def task_state(b):
        request = lax.rem(b, blocks) * part + lax.rem(iota((1, COLS), 1), part)
        return m_ref[b][:1], acc_ref[b], request < matched

    @pl.when(task_blocks > 0)
    def _():
        stages(tk, vtt, task_where, task_state, keep, task_blocks, kv)

    pay[:, lanes:] = jnp.zeros((everyone, HD), BF)

    def emit(b, _):
        g = b // blocks
        at = pl.ds(pl.multiple_of(lax.rem(b, blocks) * part, part), part)
        acc = acc_ref[b]
        turned = acc[:HD].T.astype(BF)
        both = [x.astype(F32) for x in split3(m_ref[b][:1]) + split3(acc[HD : HD + 1])]
        stats = jnp.concatenate(both + [jnp.zeros((2, COLS), F32)], 0)
        stats = jnp.concatenate([stats] * (HD // 8), 0).T
        place = pay[at, lanes:].astype(F32)
        lane_head = iota((part, HD), 1) // 8
        for h in range(group):
            head = g * group + h
            pay[at, pl.ds(pl.multiple_of(head * HD, HD), HD)] = turned[h * part : (h + 1) * part]
            place = jnp.where(lane_head == head, stats[h * part : (h + 1) * part], place)
        pay[at, lanes:] = place.astype(BF)
        return 0

    lax.fori_loop(0, kv * blocks, emit, 0, unroll=EMIT)
    homes = list(range(0, sources, 2)) + list(range(1, sources, 2))
    from_sorted = jnp.concatenate(
        [back[pl.ds(pl.multiple_of((me ^ j) * rows, rows), rows), :] for j in homes], 0
    )
    for c in range(0, lanes + HD, 2 * HD):
        end = min(c + 2 * HD, lanes + HD)
        ready = dot_nn(from_sorted, pay[:, c:end]).astype(BF)
        own_out[:, c:end] = ready[: everyone // 2]
        sent_out[:, c:end] = ready[everyone // 2 :]
    for fetch in fetches:
        fetch.wait()


def prefix(task_of, pieces, ck, vtc, tk, vtt, weight, kv, group):
    sources = len(pieces)
    rows, lanes = pieces[0].shape
    everyone = sources * rows
    blocks = everyone * group // COLS
    vmem = pl.BlockSpec(memory_space=pltpu.VMEM)
    return pl.pallas_call(
        functools.partial(prefix_kernel, sources=sources, rows=rows, kv=kv, group=group),
        in_specs=[vmem] * (5 + sources) + [pl.BlockSpec(memory_space=pltpu.HBM)],
        out_specs=[vmem] * (2 + CHUNKS),
        out_shape=[jax.ShapeDtypeStruct((everyone // 2, lanes + HD), BF)] * 2
        + [pltpu.VMEM((weight.shape[0] // CHUNKS, weight.shape[1]), BF)] * CHUNKS,
        scratch_shapes=[
            pltpu.VMEM((everyone, lanes), BF),
            pltpu.VMEM((kv * blocks, COLS, 2 * HD), BF),
            pltpu.VMEM((2, STEP, COLS), F32),
            pltpu.VMEM((kv * blocks, AUG, COLS), F32),
            pltpu.VMEM((kv * blocks, 8, COLS), F32),
            pltpu.VMEM((everyone, lanes + HD), BF),
            pltpu.VMEM((everyone, everyone), BF),
            pltpu.SemaphoreType.DMA((CHUNKS,)),
        ],
        compiler_params=pltpu.CompilerParams(vmem_limit_bytes=7 * 2**20),
        name="prefix",
    )(task_of[None, :], *pieces, ck, vtc, tk, vtt, weight)


def widen(x, head):
    return jnp.broadcast_to(x[:, 8 * head : 8 * head + 1], (x.shape[0], HD))


def pickers():
    row, col = iota((HD, HD), 0), iota((HD, HD), 1)
    same = row // 8 == col // 8
    return (same & (row % 8 < 3)).astype(BF), (same & (row % 8 >= 3) & (row % 8 < 6)).astype(BF)


def merge_kernel(a_ref, b_ref, *outs):
    rows, wide = a_ref.shape
    lanes = wide - HD
    part = rows // len(outs)
    take_m, take_l = pickers()
    sa, sb = a_ref[:, lanes:], b_ref[:, lanes:]
    ma, mb = dot_nn(sa, take_m), dot_nn(sb, take_m)
    peak = jnp.maximum(ma, mb)
    fa, fb = jnp.exp2(ma - peak), jnp.exp2(mb - peak)
    total = dot_nn(sa, take_l) * fa + dot_nn(sb, take_l) * fb

    for h in range(lanes // HD):
        at = slice(h * HD, (h + 1) * HD)
        mixed = a_ref[:, at].astype(F32) * widen(fa, h) + b_ref[:, at].astype(F32) * widen(fb, h)
        mixed = mixed.astype(BF)
        for j, ref in enumerate(outs):
            ref[:, at] = mixed[j * part : (j + 1) * part]
    place = iota(peak.shape, 1) % 8
    stats = jnp.zeros(peak.shape, F32)
    for i, x in enumerate(split3(peak) + split3(total)):
        stats = jnp.where(place == i, x.astype(F32), stats)
    stats = stats.astype(BF)
    for j, ref in enumerate(outs):
        ref[:, lanes:] = stats[j * part : (j + 1) * part]


def merge(a, b, pieces):
    shape = jax.ShapeDtypeStruct((a.shape[0] // pieces, a.shape[1]), BF)
    vmem = pl.BlockSpec(memory_space=pltpu.VMEM)
    return pl.pallas_call(
        merge_kernel,
        in_specs=[vmem] * 2,
        out_specs=[vmem] * pieces,
        out_shape=[shape] * pieces,
        compiler_params=pltpu.CompilerParams(vmem_limit_bytes=3 * 2**20),
        name="merge",
    )(a, b)


def product(bit, x, w_refs, o_ref):
    columns = o_ref.shape[1]
    at = pl.ds(pl.multiple_of((lax.axis_index("kvh") ^ bit) * columns, columns), columns)
    y = None
    for i, w_ref in enumerate(w_refs):
        tall = w_ref.shape[0]
        part = dot_nn(x[:, i * tall : (i + 1) * tall], w_ref[:, at])
        y = part if y is None else y + part
    o_ref[...] = y.astype(o_ref.dtype)


def combine_kernel(*refs, sources, bit):
    parts = refs[:sources]
    early, late = refs[sources : sources + 3], refs[sources + 3 : sources + 6]
    ho, hm, hl = [jnp.concatenate([a[...], b[...]], 0) for a, b in zip(early, late)]
    w_refs = refs[sources + 6 : -2]
    out, y_ref = refs[-2:]
    lanes = out.shape[1]
    take_m, take_l = pickers()
    tops = [dot_nn(x[:, lanes:], take_m) for x in parts]
    peak = functools.reduce(jnp.maximum, tops)
    factors = [jnp.exp2(top - peak) for top in tops]
    total = sum(dot_nn(x[:, lanes:], take_l) * factor for x, factor in zip(parts, factors))
    pieces = []
    for h in range(lanes // HD):
        at = slice(h * HD, (h + 1) * HD)
        num = sum(x[:, at].astype(F32) * widen(factor, h) for x, factor in zip(parts, factors))
        far = widen(peak, h)
        top = jnp.maximum(far, hm[:, at])
        far, near = jnp.exp2(far - top), jnp.exp2(hm[:, at] - top)
        num = num * far + ho[:, at] * near
        den = widen(total, h) * far + hl[:, at] * near
        pieces.append((num / den).astype(BF))
    attended = jnp.concatenate(pieces, 1)
    out[...] = attended
    product(bit, attended, w_refs, y_ref)


def project_kernel(x_ref, *refs, bit):
    product(bit, x_ref[...], refs[:-1], refs[-1])


def with_weight(kernel, operands, weight, shapes):
    vmem = pl.BlockSpec(memory_space=pltpu.VMEM)
    out = pl.pallas_call(
        kernel,
        in_specs=[vmem] * (len(operands) + len(weight)),
        out_specs=[vmem] * len(shapes),
        out_shape=shapes,
        compiler_params=pltpu.CompilerParams(vmem_limit_bytes=2 * 2**20),
    )(*operands, *weight)
    return out


def shards(
    queries,
    corpus_keys,
    corpus_values,
    task_keys,
    task_values,
    history_keys,
    history_values,
    history_lengths,
    task_of,
    out_weight,
):
    kv = corpus_keys.shape[1] // HD
    group = queries.shape[1] // HD // kv
    nreq, nkvh = lax.axis_size("req"), lax.axis_size("kvh")

    def swap(x, axis, size, bit):
        return lax.ppermute(x, axis, [(i, i ^ bit) for i in range(size)])

    pieces = [queries] + [None] * (nreq - 1)
    for bit in chip_order(nreq, GATHER):
        pieces[bit] = swap(queries, "req", nreq, bit)

    def part_of_history(part):
        return history(queries, history_keys, history_values, history_lengths, part, 2, kv, group)

    early = part_of_history(0)
    passed, early = lax.optimization_barrier((pieces[::2], early))
    for i, piece in enumerate(passed):
        pieces[2 * i] = piece
        pieces[2 * i + 1] = swap(piece, "req", nreq, 1)
    vtc, vtt = turn((corpus_values, task_values), kv)

    own, sent, *weight = prefix(
        task_of, pieces, corpus_keys, vtc, task_keys, vtt, out_weight, kv, group
    )
    parts = list(merge(own, swap(sent, "req", nreq, 1), nreq // 2))
    late = part_of_history(1)
    for j in range(nreq // 2 - 1, 0, -1):
        parts[j] = swap(parts[j], "req", nreq, 2 * j)

    rows = queries.shape[0]
    columns = out_weight.shape[1] // nkvh
    attended = None
    came = []
    for bit in order(nkvh, SEND) + [0]:
        shape = jax.ShapeDtypeStruct((rows, columns), BF if bit else F32)
        if attended is None:
            attended, y = with_weight(
                functools.partial(combine_kernel, sources=len(parts), bit=bit),
                parts + list(early) + list(late),
                weight,
                [jax.ShapeDtypeStruct(queries.shape, BF), shape],
            )
        else:
            kernel = functools.partial(project_kernel, bit=bit)
            (y,) = with_weight(kernel, [attended], weight, [shape])
        came.append(swap(y, "kvh", nkvh, bit) if bit else y)
    total = came[-1]
    for y in came[:-1]:
        total = total + y.astype(F32)
    return total.astype(BF)


def solution(mesh):
    return jax.shard_map(
        shards,
        mesh=mesh,
        in_specs=(
            P("req", "kvh"),
            P("req", "kvh"),
            P("req", "kvh"),
            P("req", "kvh"),
            P("req", "kvh"),
            P("req", "kvh"),
            P("req", "kvh"),
            P("req"),
            P(),
            P("kvh", None),
        ),
        out_specs=P("req", "kvh"),
        check_vma=False,
    )
```

```python
import functools
import math

import jax
import jax.numpy as jnp
from jax import lax
from jax.experimental import pallas as pl
from jax.experimental.pallas import tpu as pltpu
from jax.sharding import PartitionSpec as P


HD = 128
HOLDERS = 2
LOG2 = math.log2(math.e) / math.sqrt(HD)
BIG = 1e30
COLS = 256
STEP = 1024
SUB = 512
CHUNKS = 8
UNROLL = 4
EMIT = 4
AUG = 144
BF = jnp.bfloat16
F32 = jnp.float32


def dot_nt(a, b):
    return lax.dot_general(a, b, (((1,), (1,)), ((), ())), preferred_element_type=F32)


def dot_nn(a, b):
    return lax.dot_general(a, b, (((1,), (0,)), ((), ())), preferred_element_type=F32)


GATHER = (6, 4, 2)
SEND = (3, 2, 1)


def order(size, first):
    first = [bit for bit in first if bit < size]
    return first + [bit for bit in range(1, size) if bit not in first]


def chip_order(size, first):
    return [2 * bit for bit in order(size // 2, [bit // 2 for bit in first])]


def split3(x):
    first = x.astype(BF)
    rest = x - first.astype(F32)
    second = rest.astype(BF)
    third = (rest - second.astype(F32)).astype(BF)
    return first, second, third


def iota(shape, axis):
    return lax.broadcasted_iota(jnp.int32, shape, axis)


def history_kernel(
    len_any, q_any, k_any, v_any, o_ref, m_ref, l_ref, lengths, queries, q32, kbuf, vbuf, sems,
    *, first, waves, hist, kv, group
):
    heads = kv * group
    rows = o_ref.shape[0]
    per = rows // waves
    tall = per * hist
    small = [
        pltpu.make_async_copy(q_any.at[first : first + rows], queries, sems.at[0, waves]),
        pltpu.make_async_copy(len_any, lengths, sems.at[1, waves]),
    ]
    copies = []
    for w in range(waves):
        source = slice(first * hist + w * tall, first * hist + (w + 1) * tall)
        target = slice(w * tall, (w + 1) * tall)
        copies.append(
            [
                pltpu.make_async_copy(src.at[source], dst.at[target], sems.at[n, w])
                for n, (src, dst) in enumerate(((k_any, kbuf), (v_any, vbuf)))
            ]
        )
    for group_of in [small] + copies:
        for copy in group_of:
            copy.start()
    for copy in small:
        copy.wait()
    q32[...] = queries[...].astype(F32)
    row = iota((heads, HD), 0)
    for w in range(waves):
        for copy in copies[w]:
            copy.wait()
        ids = range(w * per, (w + 1) * per)
        scored = []
        for i in ids:
            wide = []
            for g in range(kv):
                q = jnp.zeros((heads, HD), F32)
                for h in range(g * group, (g + 1) * group):
                    line = q32[i : i + 1, h * HD : (h + 1) * HD]
                    q = jnp.where(row == h, jnp.broadcast_to(line, (heads, HD)), q)
                wide.append(q.astype(BF))
            s = dot_nt(jnp.concatenate(wide, 1), kbuf[i * hist : (i + 1) * hist, :])
            scored.append(jnp.where(iota(s.shape, 1) < lengths[first + i], s, -BIG))
        tops = [jnp.max(s, -1, keepdims=True) * LOG2 for s in scored]
        ps = [jnp.exp2(s * LOG2 - top) for s, top in zip(scored, tops)]
        totals = [jnp.sum(p, -1, keepdims=True) for p in ps]
        for i, p, top, total in zip(ids, ps, tops, totals):
            r = dot_nn(p.astype(BF), vbuf[i * hist : (i + 1) * hist, :])
            top = jnp.broadcast_to(top, (heads, HD))
            total = jnp.broadcast_to(total, (heads, HD))
            for h in range(heads):
                g = h // group
                to = slice(h * HD, (h + 1) * HD)
                o_ref[i : i + 1, to] = r[h : h + 1, g * HD : (g + 1) * HD]
                m_ref[i : i + 1, to] = top[h : h + 1]
                l_ref[i : i + 1, to] = total[h : h + 1]


def turn_kernel(cv, tv, vtc, vtt, *, kv):
    for source, target in ((cv, vtc), (tv, vtt)):
        for g in range(kv):
            for c in range(0, source.shape[0], STEP):
                target[g, :HD, c : c + STEP] = source[c : c + STEP, g * HD : (g + 1) * HD].T
            target[g, HD:, :] = jnp.ones((AUG - HD, source.shape[0]), BF)


def turn(values, kv):
    vmem = pl.BlockSpec(memory_space=pltpu.VMEM)
    return pl.pallas_call(
        functools.partial(turn_kernel, kv=kv),
        in_specs=[vmem] * len(values),
        out_specs=[vmem] * len(values),
        out_shape=[jax.ShapeDtypeStruct((kv, AUG, x.shape[0]), BF) for x in values],
        compiler_params=pltpu.CompilerParams(vmem_limit_bytes=4 * 2**20),
        name="turn",
    )(*values)


def history(queries, keys, values, lengths, part, parts, kv, group):
    rows, lanes = queries.shape[0] // parts, queries.shape[1]
    hist = keys.shape[0] // queries.shape[0]
    waves = rows // math.gcd(rows, 4)
    shape = jax.ShapeDtypeStruct((rows, lanes), F32)
    vmem = pl.BlockSpec(memory_space=pltpu.VMEM)
    operands = [lengths, queries, keys, values]
    return pl.pallas_call(
        functools.partial(
            history_kernel,
            first=part * rows,
            waves=waves,
            hist=hist,
            kv=kv,
            group=group,
        ),
        in_specs=[pl.BlockSpec(memory_space=pltpu.HBM)] * len(operands),
        out_specs=[vmem] * 3,
        scratch_shapes=[
            pltpu.SMEM(lengths.shape, jnp.int32),
            pltpu.VMEM((rows, lanes), BF),
            pltpu.VMEM((rows, lanes), F32),
        ]
        + [pltpu.VMEM((rows * hist, kv * HD), BF)] * 2
        + [pltpu.SemaphoreType.DMA((2, waves + 1))],
        out_shape=[shape] * 3,
        compiler_params=pltpu.CompilerParams(vmem_limit_bytes=6 * 2**20),
        cost_estimate=pl.CostEstimate(
            flops=4 * rows * lanes * hist * kv,
            bytes_accessed=4 * rows * hist * kv * HD,
            transcendentals=0,
        ),
        name="history",
    )(*[pltpu.with_memory_space_constraint(x, pltpu.HBM) for x in operands])


def prefix_kernel(*refs, sources, rows, kv, group):
    task_row = refs[0]
    pieces = refs[1 : 1 + sources]
    ck, vtc, tk, vtt, weight = refs[1 + sources : 6 + sources]
    own_out, sent_out = refs[6 + sources : 8 + sources]
    kept = refs[8 + sources : 8 + sources + CHUNKS]
    q_all, qs, s_ref, acc_ref, m_ref, pay, back, sems = refs[8 + sources + CHUNKS :]
    tall = weight.shape[0] // CHUNKS
    fetches = [
        pltpu.make_async_copy(
            weight.at[i * tall : (i + 1) * tall], kept[i], sems.at[i]
        )
        for i in range(CHUNKS)
    ]
    for fetch in fetches:
        fetch.start()
    me = lax.axis_index("req")
    my_task = me // HOLDERS
    heads = kv * group
    lanes = heads * HD
    everyone = sources * rows
    part = COLS // group
    blocks = everyone // part

    square = (everyone, everyone)
    match = jnp.broadcast_to(task_row[...], (8, everyone)) == my_task
    count = dot_nn(match.astype(BF), (iota(square, 0) <= iota(square, 1)).astype(BF))
    live = jnp.sum(match.astype(F32), 1, keepdims=True)
    slot = jnp.where(match, count - 1.0, live + iota(count.shape, 1).astype(F32) - count)
    hot = (iota(square, 0) == slot[:1].astype(jnp.int32)).astype(F32)
    to_sorted = hot.astype(BF)
    back[...] = hot.T.astype(BF)
    matched = jnp.sum((task_row[...] == my_task).astype(jnp.int32))
    task_blocks = (matched + part - 1) // part

    for j in range(sources):
        q_all[pl.ds(pl.multiple_of((me ^ j) * rows, rows), rows), :] = pieces[j][...]
    for g in range(kv):
        for h in range(group):
            at = (g * group + h) * HD
            if h % 2 == 0:
                both = dot_nn(to_sorted, q_all[:, at : at + 2 * HD]) * LOG2
            x = both[:, (h % 2) * HD : (h % 2 + 1) * HD]
            high = x.astype(BF)
            low = (x - high.astype(F32)).astype(BF)
            for b in range(blocks):
                qs[g * blocks + b, h * part : (h + 1) * part, :HD] = high[b * part : (b + 1) * part]
                qs[g * blocks + b, h * part : (h + 1) * part, HD:] = low[b * part : (b + 1) * part]

    def lane(g):
        return pl.ds(pl.multiple_of(g * HD, HD), HD)

    def scores(keys, start, g, index):
        k = keys[start : start + SUB, lane(g)]
        return dot_nt(jnp.concatenate([k, k], 1), qs[index])

    def fold(x, m8):
        x = jnp.max(x.reshape(-1, 8, COLS), 0)
        return x if m8 is None else jnp.maximum(m8, x)

    def stages(keys, vt, where_of, first_state, finish, turns, inner):
        n = keys.shape[0] // STEP

        def head(slot):
            b, g = where_of(0, 0)
            m8 = None
            for c in range(0, STEP, SUB):
                s = scores(keys, c, g, b)
                s_ref[slot, c : c + SUB] = s
                m8 = fold(s, m8)
            return m8

        def one(i, u, m8):
            b, g = where_of(i, u)
            last = u + 1 == inner
            b_next, g_next = where_of(jnp.minimum(i + 1, turns - 1) if last else i, 0 if last else u + 1)
            m, acc, valid = first_state(b)
            for stage in range(n):
                now, later = stage % 2, (stage + 1) % 2
                top = jnp.max(m8, 0, keepdims=True)
                new = top if m is None else jnp.maximum(m, top)
                if valid is not None:
                    new = jnp.where(valid, new, m)
                    shift = jnp.where(valid, new, BIG)
                else:
                    shift = new
                m8 = None
                r = None
                for c in range(0, STEP, SUB):
                    if stage + 1 < n:
                        s = scores(keys, (stage + 1) * STEP + c, g, b)
                    else:
                        s = scores(keys, c, g_next, b_next)
                    s_ref[later, c : c + SUB] = s
                    m8 = fold(s, m8)
                    p = jnp.exp2(s_ref[now, c : c + SUB] - shift).astype(BF)
                    at = stage * STEP + c
                    y = dot_nn(vt[g, :, at : at + SUB], p)
                    r = y if r is None else r + y
                acc = r if acc is None else acc * jnp.exp2(m - new) + r
                m = new
            finish(b, m, acc)
            return m8

        def body(i, m8):
            for u in range(inner):
                m8 = one(i, u, m8)
            return m8

        lax.fori_loop(0, turns, body, head(0))

    def keep(b, m, acc):
        acc_ref[b] = acc
        m_ref[b] = jnp.broadcast_to(m, (8, COLS))

    def corpus_where(i, u):
        item = i * inner + u
        return item, item // blocks

    inner = math.gcd(UNROLL, kv * blocks)
    stages(ck, vtc, corpus_where, lambda b: (None, None, None), keep, kv * blocks // inner, inner)

    def task_where(i, u):
        return u * blocks + i, u

    def task_state(b):
        request = lax.rem(b, blocks) * part + lax.rem(iota((1, COLS), 1), part)
        return m_ref[b][:1], acc_ref[b], request < matched

    @pl.when(task_blocks > 0)
    def _():
        stages(tk, vtt, task_where, task_state, keep, task_blocks, kv)

    pay[:, lanes:] = jnp.zeros((everyone, HD), BF)

    def emit(b, _):
        g = b // blocks
        at = pl.ds(pl.multiple_of(lax.rem(b, blocks) * part, part), part)
        acc = acc_ref[b]
        turned = acc[:HD].T.astype(BF)
        both = [x.astype(F32) for x in split3(m_ref[b][:1]) + split3(acc[HD : HD + 1])]
        stats = jnp.concatenate(both + [jnp.zeros((2, COLS), F32)], 0)
        stats = jnp.concatenate([stats] * (HD // 8), 0).T
        place = pay[at, lanes:].astype(F32)
        lane_head = iota((part, HD), 1) // 8
        for h in range(group):
            head = g * group + h
            pay[at, pl.ds(pl.multiple_of(head * HD, HD), HD)] = turned[h * part : (h + 1) * part]
            place = jnp.where(lane_head == head, stats[h * part : (h + 1) * part], place)
        pay[at, lanes:] = place.astype(BF)
        return 0

    lax.fori_loop(0, kv * blocks, emit, 0, unroll=EMIT)
    homes = list(range(0, sources, 2)) + list(range(1, sources, 2))
    from_sorted = jnp.concatenate(
        [back[pl.ds(pl.multiple_of((me ^ j) * rows, rows), rows), :] for j in homes], 0
    )
    for c in range(0, lanes + HD, 2 * HD):
        end = min(c + 2 * HD, lanes + HD)
        ready = dot_nn(from_sorted, pay[:, c:end]).astype(BF)
        own_out[:, c:end] = ready[: everyone // 2]
        sent_out[:, c:end] = ready[everyone // 2 :]
    for fetch in fetches:
        fetch.wait()


def prefix(task_of, pieces, ck, vtc, tk, vtt, weight, kv, group):
    sources = len(pieces)
    rows, lanes = pieces[0].shape
    everyone = sources * rows
    blocks = everyone * group // COLS
    vmem = pl.BlockSpec(memory_space=pltpu.VMEM)
    return pl.pallas_call(
        functools.partial(prefix_kernel, sources=sources, rows=rows, kv=kv, group=group),
        in_specs=[vmem] * (5 + sources) + [pl.BlockSpec(memory_space=pltpu.HBM)],
        out_specs=[vmem] * (2 + CHUNKS),
        out_shape=[jax.ShapeDtypeStruct((everyone // 2, lanes + HD), BF)] * 2
        + [pltpu.VMEM((weight.shape[0] // CHUNKS, weight.shape[1]), BF)] * CHUNKS,
        scratch_shapes=[
            pltpu.VMEM((everyone, lanes), BF),
            pltpu.VMEM((kv * blocks, COLS, 2 * HD), BF),
            pltpu.VMEM((2, STEP, COLS), F32),
            pltpu.VMEM((kv * blocks, AUG, COLS), F32),
            pltpu.VMEM((kv * blocks, 8, COLS), F32),
            pltpu.VMEM((everyone, lanes + HD), BF),
            pltpu.VMEM((everyone, everyone), BF),
            pltpu.SemaphoreType.DMA((CHUNKS,)),
        ],
        compiler_params=pltpu.CompilerParams(vmem_limit_bytes=7 * 2**20),
        name="prefix",
    )(task_of[None, :], *pieces, ck, vtc, tk, vtt, weight)


def widen(x, head):
    return jnp.broadcast_to(x[:, 8 * head : 8 * head + 1], (x.shape[0], HD))


def pickers():
    row, col = iota((HD, HD), 0), iota((HD, HD), 1)
    same = row // 8 == col // 8
    return (same & (row % 8 < 3)).astype(BF), (same & (row % 8 >= 3) & (row % 8 < 6)).astype(BF)


def merge_kernel(a_ref, b_ref, *outs):
    rows, wide = a_ref.shape
    lanes = wide - HD
    part = rows // len(outs)
    take_m, take_l = pickers()
    sa, sb = a_ref[:, lanes:], b_ref[:, lanes:]
    ma, mb = dot_nn(sa, take_m), dot_nn(sb, take_m)
    peak = jnp.maximum(ma, mb)
    fa, fb = jnp.exp2(ma - peak), jnp.exp2(mb - peak)
    total = dot_nn(sa, take_l) * fa + dot_nn(sb, take_l) * fb

    for h in range(lanes // HD):
        at = slice(h * HD, (h + 1) * HD)
        mixed = a_ref[:, at].astype(F32) * widen(fa, h) + b_ref[:, at].astype(F32) * widen(fb, h)
        mixed = mixed.astype(BF)
        for j, ref in enumerate(outs):
            ref[:, at] = mixed[j * part : (j + 1) * part]
    place = iota(peak.shape, 1) % 8
    stats = jnp.zeros(peak.shape, F32)
    for i, x in enumerate(split3(peak) + split3(total)):
        stats = jnp.where(place == i, x.astype(F32), stats)
    stats = stats.astype(BF)
    for j, ref in enumerate(outs):
        ref[:, lanes:] = stats[j * part : (j + 1) * part]


def merge(a, b, pieces):
    shape = jax.ShapeDtypeStruct((a.shape[0] // pieces, a.shape[1]), BF)
    vmem = pl.BlockSpec(memory_space=pltpu.VMEM)
    return pl.pallas_call(
        merge_kernel,
        in_specs=[vmem] * 2,
        out_specs=[vmem] * pieces,
        out_shape=[shape] * pieces,
        compiler_params=pltpu.CompilerParams(vmem_limit_bytes=3 * 2**20),
        name="merge",
    )(a, b)


def product(bit, x, w_refs, o_ref):
    columns = o_ref.shape[1]
    at = pl.ds(pl.multiple_of((lax.axis_index("kvh") ^ bit) * columns, columns), columns)
    y = None
    for i, w_ref in enumerate(w_refs):
        tall = w_ref.shape[0]
        part = dot_nn(x[:, i * tall : (i + 1) * tall], w_ref[:, at])
        y = part if y is None else y + part
    o_ref[...] = y.astype(o_ref.dtype)


def combine_kernel(*refs, sources, bit):
    parts = refs[:sources]
    early, late = refs[sources : sources + 3], refs[sources + 3 : sources + 6]
    ho, hm, hl = [jnp.concatenate([a[...], b[...]], 0) for a, b in zip(early, late)]
    w_refs = refs[sources + 6 : -2]
    out, y_ref = refs[-2:]
    lanes = out.shape[1]
    take_m, take_l = pickers()
    tops = [dot_nn(x[:, lanes:], take_m) for x in parts]
    peak = functools.reduce(jnp.maximum, tops)
    factors = [jnp.exp2(top - peak) for top in tops]
    total = sum(dot_nn(x[:, lanes:], take_l) * factor for x, factor in zip(parts, factors))
    pieces = []
    for h in range(lanes // HD):
        at = slice(h * HD, (h + 1) * HD)
        num = sum(x[:, at].astype(F32) * widen(factor, h) for x, factor in zip(parts, factors))
        far = widen(peak, h)
        top = jnp.maximum(far, hm[:, at])
        far, near = jnp.exp2(far - top), jnp.exp2(hm[:, at] - top)
        num = num * far + ho[:, at] * near
        den = widen(total, h) * far + hl[:, at] * near
        pieces.append((num / den).astype(BF))
    attended = jnp.concatenate(pieces, 1)
    out[...] = attended
    product(bit, attended, w_refs, y_ref)


def project_kernel(x_ref, *refs, bit):
    product(bit, x_ref[...], refs[:-1], refs[-1])


def with_weight(kernel, operands, weight, shapes):
    vmem = pl.BlockSpec(memory_space=pltpu.VMEM)
    out = pl.pallas_call(
        kernel,
        in_specs=[vmem] * (len(operands) + len(weight)),
        out_specs=[vmem] * len(shapes),
        out_shape=shapes,
        compiler_params=pltpu.CompilerParams(vmem_limit_bytes=2 * 2**20),
    )(*operands, *weight)
    return out


def finish_kernel(*refs):
    total = refs[0][...]
    for y in refs[1:-1]:
        total = total + y[...].astype(F32)
    refs[-1][...] = total.astype(BF)


def finish(own, came):
    vmem = pl.BlockSpec(memory_space=pltpu.VMEM)
    return pl.pallas_call(
        finish_kernel,
        grid=(1,),
        in_specs=[vmem] * (1 + len(came)),
        out_specs=pl.BlockSpec(own.shape, lambda i: (0, 0)),
        out_shape=jax.ShapeDtypeStruct(own.shape, BF),
        compiler_params=pltpu.CompilerParams(vmem_limit_bytes=2 * 2**20),
        name="finish",
    )(own, *came)


def shards(
    queries,
    corpus_keys,
    corpus_values,
    task_keys,
    task_values,
    history_keys,
    history_values,
    history_lengths,
    task_of,
    out_weight,
):
    kv = corpus_keys.shape[1] // HD
    group = queries.shape[1] // HD // kv
    nreq, nkvh = lax.axis_size("req"), lax.axis_size("kvh")

    def swap(x, axis, size, bit):
        return lax.ppermute(x, axis, [(i, i ^ bit) for i in range(size)])

    pieces = [queries] + [None] * (nreq - 1)
    for bit in chip_order(nreq, GATHER):
        pieces[bit] = swap(queries, "req", nreq, bit)

    def part_of_history(part):
        return history(queries, history_keys, history_values, history_lengths, part, 2, kv, group)

    early = part_of_history(0)
    passed, early = lax.optimization_barrier((pieces[::2], early))
    for i, piece in enumerate(passed):
        pieces[2 * i] = piece
        pieces[2 * i + 1] = swap(piece, "req", nreq, 1)
    vtc, vtt = turn((corpus_values, task_values), kv)

    own, sent, *weight = prefix(
        task_of, pieces, corpus_keys, vtc, task_keys, vtt, out_weight, kv, group
    )
    parts = list(merge(own, swap(sent, "req", nreq, 1), nreq // 2))
    late = part_of_history(1)
    for j in range(nreq // 2 - 1, 0, -1):
        parts[j] = swap(parts[j], "req", nreq, 2 * j)

    rows = queries.shape[0]
    columns = out_weight.shape[1] // nkvh
    attended = None
    came = []
    for bit in order(nkvh, SEND) + [0]:
        shape = jax.ShapeDtypeStruct((rows, columns), BF if bit else F32)
        if attended is None:
            attended, y = with_weight(
                functools.partial(combine_kernel, sources=len(parts), bit=bit),
                parts + list(early) + list(late),
                weight,
                [jax.ShapeDtypeStruct(queries.shape, BF), shape],
            )
        else:
            kernel = functools.partial(project_kernel, bit=bit)
            (y,) = with_weight(kernel, [attended], weight, [shape])
        came.append(swap(y, "kvh", nkvh, bit) if bit else y)
    return finish(came[-1], came[:-1])


def solution(mesh):
    return jax.shard_map(
        shards,
        mesh=mesh,
        in_specs=(
            P("req", "kvh"),
            P("req", "kvh"),
            P("req", "kvh"),
            P("req", "kvh"),
            P("req", "kvh"),
            P("req", "kvh"),
            P("req", "kvh"),
            P("req"),
            P(),
            P("kvh", None),
        ),
        out_specs=P("req", "kvh"),
        check_vma=False,
    )
```
